256 devices in a mesh: gz: 16 (over x, y_hi, core), ta: 16 (over z, y_lo).
Axes of the slice: x: 4, y: 4 (y_hi: 2, y_lo: 2; y = y_hi * 2 + y_lo), z: 8, core: 2. Of those that a mesh axis runs over, the one named last changes fastest.
Arguments:
- base_links: float32 [4, 2, 3, 3, 32, 32, 128], P(None, None, None, None, 'gz', 'ta'), may hold values from -6 to 6
- smeared_links: float32 [4, 2, 3, 3, 32, 32, 128], P(None, None, None, None, 'gz', 'ta'), may hold values from -6 to 6
- top_force: float32 [4, 2, 3, 3, 32, 32, 128], P(None, None, None, None, 'gz', 'ta'), may hold values from -6 to 6
Outputs:
- base_force: float32 [4, 2, 3, 3, 32, 32, 128], P(None, None, None, None, 'gz', 'ta')
The draws below stay inside these ranges and needn't reach their ends.
All inputs are finite; a program needn't handle non-finite values.
Results may differ from the reference program's by a relative error of at most 0.0001.
Values sent between devices are 32-bit elements; how exact they have to be, the bound alone decides.
A program may use at most 64 MiB of HBM per device.

```python
import jax
import jax.numpy as jnp
from jax import lax

LY = 8
CZ = 2
CT = 2
TERMS = 6
NZ = 32
NT = 32
XY = 128
N_GZ = 16
N_TA = 16


def block_levels(rng, extent, shards, low, high):
    gain = 1.0
    for dim, blocks in shards:
        heights = jax.random.uniform(jax.random.fold_in(jax.random.fold_in(rng, 6), dim), (blocks,), jnp.float32, low / len(shards), high / len(shards))
        gain = gain * jnp.repeat(jnp.exp(heights), extent[dim] // blocks).reshape((-1,) + (1,) * (len(extent) - 1 - dim))
    return gain


def centred(key, extent, spread, most, split=(), held_as=jnp.bfloat16):
    entries = spread * jax.random.normal(key, extent, jnp.float32)
    if split:
        entries = entries * block_levels(key, extent, split, -0.22, 0.18)
    return jnp.clip(entries, -most, most).astype(held_as)


def setup_inputs(seed: int = 0) -> dict:
    keys = jax.random.split(jax.random.key(seed), 4)
    return {
        "base_links": centred(keys[0], (4, 2, 3, 3, NZ, NT, XY), 0.41, 6.0, ((4, 16), (5, 16)), jnp.float32),
        "smeared_links": centred(keys[1], (4, 2, 3, 3, NZ, NT, XY), 0.41, 6.0, ((4, 16), (5, 16)), jnp.float32),
        "top_force": centred(keys[2], (4, 2, 3, 3, NZ, NT, XY), 1.0, 6.0, ((4, 16), (5, 16)), jnp.float32),
    }


smear_weight = 0.1
unit_steps = ((0, 0, 1, 0), (0, 0, 0, 1), (1, 0, 0, 0), (0, 1, 0, 0))

def real_product(left_part, right_part):
    return lax.optimization_barrier(jnp.sum(left_part[:, :, None] * right_part[None, :, :], axis=1))

def complex_product(left_factor, right_factor):
    real_out = real_product(left_factor[0], right_factor[0]) - real_product(left_factor[1], right_factor[1])
    imag_out = real_product(left_factor[0], right_factor[1]) + real_product(left_factor[1], right_factor[0])
    return jnp.stack([real_out, imag_out])

def adjoint(matrices):
    return jnp.stack([jnp.swapaxes(matrices[0], 0, 1), -jnp.swapaxes(matrices[1], 0, 1)])

def shift_sites(window, step_x, step_y):
    if step_x != 0:
        window = jnp.roll(window, -step_x * LY, axis=-1)
    if step_y != 0:
        position = lax.iota(jnp.int32, window.shape[-1]) % LY
        inside = jnp.roll(window, -step_y, axis=-1)
        wrapped = jnp.roll(window, step_y * (LY - 1), axis=-1)
        if step_y > 0:
            at_edge = position == LY - 1
        else:
            at_edge = position == 0
        window = jnp.where(at_edge, wrapped, inside)
    return window

def moved(matrices, offset):
    step_z, step_t, step_x, step_y = offset
    rows_padded = matrices.shape[3]
    cols_padded = matrices.shape[4]
    window = matrices[:, :, :, 1 + step_z:rows_padded - 1 + step_z, 1 + step_t:cols_padded - 1 + step_t, :]
    return shift_sites(window, step_x, step_y)

def combine(first, second, factor):
    return tuple((a + factor * b for a, b in zip(first, second)))

def stout_step(link_field):
    anchor = (0, 0, 0, 0)
    results = []
    for along in range(4):
        step_along = unit_steps[along]
        staple_sum = None
        for across in range(4):
            if across == along:
                continue
            step_across = unit_steps[across]
            upper_loop = complex_product(complex_product(moved(link_field[across], anchor), moved(link_field[along], step_across)), adjoint(moved(link_field[across], step_along)))
            back = combine(anchor, step_across, -1)
            lower_loop = complex_product(complex_product(adjoint(moved(link_field[across], back)), moved(link_field[along], back)), moved(link_field[across], combine(step_along, step_across, -1)))
            term = upper_loop + lower_loop
            staple_sum = term if staple_sum is None else staple_sum + term
        link_here = moved(link_field[along], anchor)
        omega_term = smear_weight * complex_product(staple_sum, adjoint(link_here))
        skew_part = 0.5 * (omega_term - adjoint(omega_term))
        trace_part = skew_part[:, 0, 0] + skew_part[:, 1, 1] + skew_part[:, 2, 2]
        unit_matrix = jnp.stack([jnp.eye(3, dtype=link_field.dtype), jnp.zeros((3, 3), link_field.dtype)])
        unit_matrix = unit_matrix.reshape((2, 3, 3, 1, 1, 1))
        generator = skew_part - trace_part[:, None, None] / 3.0 * unit_matrix
        exponent = jnp.broadcast_to(unit_matrix, generator.shape)
        for degree in range(TERMS, 0, -1):
            exponent = unit_matrix + complex_product(generator, exponent) / degree
        results.append(complex_product(exponent, link_here))
    return jnp.stack(results)

def fold_rims(accumulated):
    middle = accumulated[..., 1:-1, :, :]
    middle = jnp.concatenate([middle[..., :1, :, :] + accumulated[..., -1:, :, :], middle[..., 1:, :, :]], axis=4)
    middle = jnp.concatenate([middle[..., :-1, :, :], middle[..., -1:, :, :] + accumulated[..., :1, :, :]], axis=4)
    owned = middle[..., 1:-1, :]
    owned = jnp.concatenate([owned[..., :1, :] + middle[..., -1:, :], owned[..., 1:, :]], axis=5)
    owned = jnp.concatenate([owned[..., :-1, :], owned[..., -1:, :] + middle[..., :1, :]], axis=5)
    return owned

def level_back(link_field, force_field):
    wrap_t = jnp.concatenate([link_field[..., -1:, :], link_field, link_field[..., :1, :]], axis=5)
    wrap_zt = jnp.concatenate([wrap_t[..., -1:, :, :], wrap_t, wrap_t[..., :1, :, :]], axis=4)
    start_acc = jnp.zeros(wrap_zt.shape, link_field.dtype)

    def visit_block(block_index, accumulated):
        row_start = (block_index // N_TA * CZ).astype(jnp.int32)
        col_start = (block_index % N_TA * CT).astype(jnp.int32)
        anchor = row_start * 0
        corner = (anchor, anchor, anchor, anchor, row_start, col_start, anchor)
        block_links = lax.dynamic_slice(wrap_zt, corner, (4, 2, 3, 3, CZ + 2, CT + 2, XY))
        block_force = lax.dynamic_slice(force_field, corner, (4, 2, 3, 3, CZ, CT, XY))
        _, pullback = jax.vjp(stout_step, block_links)
        cotangent, = pullback(block_force)
        previous = lax.dynamic_slice(accumulated, corner, (4, 2, 3, 3, CZ + 2, CT + 2, XY))
        return lax.dynamic_update_slice(accumulated, previous + cotangent, corner)
    accumulated = lax.fori_loop(0, N_GZ * N_TA, visit_block, start_acc)
    return fold_rims(accumulated)

def reference(base_links, smeared_links, top_force):
    mid_force = level_back(smeared_links, top_force)
    return level_back(base_links, mid_force)
```

```python
import jax
import jax.numpy as jnp
from jax import lax
from jax.experimental import pallas as pl
from jax.experimental.pallas import tpu as pltpu
from jax.sharding import PartitionSpec as P

MESH = pl.DeviceIdType.MESH
LY = 8
WEIGHT = 0.1
LANES = 128
LINK = 18
SKEW = 9


def masks():
    row = lax.broadcasted_iota(jnp.int32, (1, 8, LANES), 1)
    col = lax.broadcasted_iota(jnp.int32, (1, 8, LANES), 2) % LY
    return {
        "low": row < 4,
        "even": row % 2 == 0,
        "near": row % 4 < 2,
        "row": row,
        "first": col == 0,
        "last": col == LY - 1,
    }


def pick(mask, yes, no):
    return jnp.where(jnp.broadcast_to(mask, yes.shape), yes, no)


def rows(v, shift):
    return pltpu.roll(v, shift % 8, 1)


def fwd_x(v):
    return pltpu.roll(v, LANES - LY, 2)


def back_x(v):
    return pltpu.roll(v, LY, 2)


def fwd_y(m, v):
    return pick(m["last"], pltpu.roll(v, LY - 1, 2), pltpu.roll(v, LANES - 1, 2))


def back_y(m, v):
    return pick(m["first"], pltpu.roll(v, LANES - LY + 1, 2), pltpu.roll(v, 1, 2))


def fwd_xy(m, v):
    return pick(m["low"], fwd_x(v), fwd_y(m, v))


def back_xy(m, v):
    return pick(m["low"], back_x(v), back_y(m, v))


def split(v):
    return v[:9].reshape(3, 3, 8, LANES), v[9:].reshape(3, 3, 8, LANES)


def join(m):
    return jnp.concatenate([m[0].reshape(9, 8, LANES), m[1].reshape(9, 8, LANES)], axis=0)


def outer_sum(lefts, rights):
    total = None
    for left, right in zip(lefts, rights):
        term = left[:, None] * right[None, :]
        total = term if total is None else total + term
    return total


def columns(a):
    return [a[:, k] for k in range(3)]


def lines(a):
    return [a[k] for k in range(3)]


def product(left, right, sl, sr):
    (ar, ai), (br, bi) = left, right
    rr, ii = outer_sum(ar, br), outer_sum(ai, bi)
    ri, ir = outer_sum(ar, bi), outer_sum(ai, br)
    re = rr - ii if sl * sr > 0 else rr + ii
    if sl > 0 and sr > 0:
        im = ri + ir
    elif sl < 0 and sr > 0:
        im = ri - ir
    else:
        im = ir - ri
    return re, im


def mul(a, b):
    return product((columns(a[0]), columns(a[1])), (lines(b[0]), lines(b[1])), 1, 1)


def mul_dn(a, b):
    return product((lines(a[0]), lines(a[1])), (lines(b[0]), lines(b[1])), -1, 1)


def mul_nd(a, b):
    return product((columns(a[0]), columns(a[1])), (columns(b[0]), columns(b[1])), 1, -1)


def add(a, b):
    return a[0] + b[0], a[1] + b[1]


def sub(a, b):
    return a[0] - b[0], a[1] - b[1]


def flip(v):
    return jnp.stack([v[:, 0], v[:, 1], v[:, 2]], axis=0)


def dagger(a):
    return flip(a[0]), -flip(a[1])


def scaled(c, a):
    cr, ci = c
    return cr * a[0] - ci * a[1], cr * a[1] + ci * a[0]


def skew_parts(a):
    re, im = a
    out = [im[0, 0], im[1, 1], im[2, 2]]
    for i, j in ((0, 1), (0, 2), (1, 2)):
        out += [0.5 * (re[i, j] - re[j, i]), 0.5 * (im[i, j] + im[j, i])]
    return out


def skew_matrix(v):
    d0, d1, d2, r01, i01, r02, i02, r12, i12 = [v[k] for k in range(9)]
    zero = jnp.zeros_like(d0)
    re = jnp.stack([jnp.stack([zero, r01, r02]), jnp.stack([-r01, zero, r12]), jnp.stack([-r02, -r12, zero])])
    im = jnp.stack([jnp.stack([d0, i01, i02]), jnp.stack([i01, d1, i12]), jnp.stack([i02, i12, d2])])
    return re, im


def pack_sends(m, low, high, comps, send):
    send[0, :comps] = pick(m["near"], rows(low, -2), high)
    send[1, :comps] = pick(m["near"], high, rows(low, 2))
    send[2, :comps] = pick(m["even"], rows(low, -1), high)
    send[3, :comps] = pick(m["even"], rows(high, 4), rows(low, 1))


def copies(src_low_high, send, recv, corner, ssem, rsem, where):
    plan = (
        (send.at[0], recv.at[0], where[0]),
        (send.at[1, :, pl.ds(2, 6)], recv.at[1, :, pl.ds(2, 6)], where[1]),
        (send.at[2], recv.at[2], where[2]),
        (send.at[3, :, pl.ds(1, 7)], recv.at[3, :, pl.ds(1, 7)], where[3]),
        (src_low_high.at[1, :, pl.ds(2, 1)], corner.at[:, pl.ds(1, 1)], where[4]),
        (src_low_high.at[1, :, pl.ds(5, 1)], corner.at[:, pl.ds(3, 1)], where[5]),
    )
    order = (1, 3, 0, 2, 4, 5)
    return [
        pltpu.make_async_remote_copy(
            src_ref=plan[k][0],
            dst_ref=plan[k][1],
            send_sem=ssem.at[k],
            recv_sem=rsem.at[k],
            device_id=plan[k][2],
            device_id_type=MESH,
        )
        for k in order
    ]


def gather_into(m, low, high, recv, corner, ga, gb, gc, gd):
    at_zm, at_zp, at_tm, at_tp = recv[0], recv[1], recv[2], recv[3]
    diag = corner[...]
    row = m["row"]
    a0 = pick(m["low"], low, rows(high, 4))
    d0 = pick(m["low"], rows(low, 4), high)
    ga[0], gd[0] = a0, d0
    gb[0] = pick(m["low"], fwd_x(d0), pick(m["near"], rows(d0, -2), rows(at_zp, 2)))
    gc[0] = pick(m["low"], fwd_y(m, a0), pick(m["even"], rows(a0, -1), rows(at_tp, 1)))
    up_z = pick(m["near"], rows(low, -2), at_zp)
    up_t = pick(m["even"], rows(low, -1), at_tp)
    ga[1], gd[1] = low, high
    gb[1] = fwd_xy(m, high)
    gc[1] = pick(m["low"], up_z, up_t)
    d2 = rows(high, 4)
    ga[2], gd[2] = low, d2
    gb[2] = fwd_xy(m, d2)
    gc[2] = pick(m["low"], up_t, up_z)
    dz = pick(row < 2, rows(at_zm, -2), pick(row < 4, at_zm, pick(row < 6, rows(at_zm, 2), rows(at_zm, 4))))
    ga[3], gd[3] = at_zm, dz
    gb[3] = pick(row < 6, fwd_xy(m, dz), pick(m["even"], rows(at_zm, 3), rows(diag, -2 + 8)))
    dt = pick(m["low"], pick(m["even"], rows(at_tm, 3), rows(at_tm, 4)), pick(m["even"], rows(at_tm, -1), at_tm))
    ga[4], gd[4] = at_tm, dt
    gb[4] = pick(m["even"], fwd_xy(m, dt), pick(row < 2, rows(at_tm, 2), diag))


def scatter_sum(m, pa, pb, pc, pd, rim):
    a0, b0, c0, d0 = pa[0], pb[0], pc[0], pd[0]
    a1, b1, c1, d1 = pa[1], pb[1], pc[1], pd[1]
    a2, b2, c2, d2 = pa[2], pb[2], pc[2], pd[2]
    rz, rt = rim[0], rim[1]
    from_z = pick(m["near"], rz, rows(pick(m["low"], c1, c2), 2))
    from_t = pick(m["even"], rt, rows(pick(m["low"], c2, c1), 1))
    low = (a1 + a2) + (from_z + from_t)
    low = low + pick(m["low"], a0 + back_y(m, c0), rows(d0 + back_x(b0), 4))
    high = (d1 + back_xy(m, b1)) + rows(d2 + back_xy(m, b2), 4)
    z_part = a0 + pick(m["even"], rows(rt, 3), rows(c0, 1))
    t_part = d0 + pick(m["near"], rows(rz, -2), rows(b0, 2))
    high = high + pick(m["low"], rows(z_part, 4), t_part)
    return low, high


def staples(ga, gb, gc, gd, keep_t, keep_z, pa, pb, pc, pd, rim):
    def block(k, carry):
        a, b, c, d = split(ga[k]), split(gb[k]), split(gc[k]), split(gd[k])
        t = mul_dn(a, d)
        keep_t[k] = join(t)
        pb[k] = join(mul(t, c))
        pc[k] = join(mul_dn(t, b))
        z = mul_nd(c, b)
        keep_z[k] = join(z)
        pa[k] = join(mul(d, z))
        pd[k] = join(mul_nd(a, z))
        return carry

    lax.fori_loop(0, 3, block, 0)

    def edge(k, carry):
        a, b, d = split(ga[k + 3]), split(gb[k + 3]), split(gd[k + 3])
        t = mul_dn(a, d)
        keep_t[k + 3] = join(t)
        rim[k] = join(mul_dn(t, b))
        return carry

    lax.fori_loop(0, 2, edge, 0)


def staple_forces(ga, gb, gc, gd, keep_t, keep_z, sa, sd, wa, wb, wc, wd, pa, pb, pc, pd, rim):
    def block(k, carry):
        a, b, c, d = split(ga[k]), split(gb[k]), split(gc[k]), split(gd[k])
        va, vd = wa[k], wd[k]
        oa, ob, oc, od = skew_matrix(va), skew_matrix(wb[k]), skew_matrix(wc[k]), skew_matrix(vd)
        t, z = split(keep_t[k]), split(keep_z[k])
        n = mul_dn(a, mul(skew_matrix(va - vd), d))
        pb[k] = join(mul(sub(mul(t, oc), n), c))
        pc[k] = join(mul(sub(mul_dn(t, ob), dagger(n)), b))
        q = sub(mul(oc, z), mul(z, ob))
        pa[k] = join(add(mul(d, q), mul(od, split(sa[k]))))
        pd[k] = join(add(mul_nd(a, q), mul(oa, split(sd[k]))))
        return carry

    lax.fori_loop(0, 3, block, 0)

    def edge(k, carry):
        a, b, d = split(ga[k + 3]), split(gb[k + 3]), split(gd[k + 3])
        n = mul_dn(a, mul(skew_matrix(wa[k + 3] - wd[k + 3]), d))
        t = split(keep_t[k + 3])
        rim[k] = join(mul(sub(mul_dn(t, skew_matrix(wb[k + 3])), dagger(n)), b))
        return carry

    lax.fori_loop(0, 2, edge, 0)


def weights(h):
    hh = h * h
    r2 = 1.0 - hh * 0.5
    r4 = r2 + hh * hh * (1.0 / 24.0)
    r6 = r4 - hh * hh * hh * (1.0 / 720.0)
    i3 = h - h * hh * (1.0 / 6.0)
    i5 = i3 + h * hh * hh * (1.0 / 120.0)
    return (r6, i5), (r4, i5), (r4, i3), (r2, i3), (r2, h)


def exponent_parts(links, staple_sum, keep_b, keep_bb, keep_e, keep_s):
    def block(k, carry):
        u, c = split(links[k]), split(staple_sum[k])
        omega = mul_nd(c, u)
        parts = [WEIGHT * v for v in skew_parts(omega)]
        h = (parts[0] + parts[1] + parts[2]) * (1.0 / 3.0)
        parts = jnp.stack([v - h for v in parts[:3]] + parts[3:])
        b = skew_matrix(parts)
        bb = mul(b, b)
        p = 0.5 * (bb[0][0, 0] + bb[0][1, 1] + bb[0][2, 2])
        s = jnp.sum((b[1] * bb[0] - b[0] * bb[1]).reshape(9, 8, LANES), axis=0) * (1.0 / 3.0)
        w0, w1, w2, w3, w4 = weights(h)
        pp, ps = p * p, p * s
        f0 = (
            w0[0] - s * w3[1] * (1.0 / 6.0) - ps * h * (1.0 / 120.0) - s * s * (1.0 / 720.0),
            w0[1] + s * w3[0] * (1.0 / 6.0) + ps * (1.0 / 120.0),
        )
        f1 = (
            w1[0] + p * w3[0] * (1.0 / 6.0) - s * w4[1] * (1.0 / 24.0) + pp * (1.0 / 120.0),
            w1[1] + p * w3[1] * (1.0 / 6.0) + s * w4[0] * (1.0 / 24.0) + pp * h * (1.0 / 120.0) + ps * (1.0 / 360.0),
        )
        f2 = (
            w2[0] * 0.5 + p * w4[0] * (1.0 / 24.0) - s * h * (1.0 / 120.0) + pp * (1.0 / 720.0),
            w2[1] * 0.5 + p * w4[1] * (1.0 / 24.0) + s * (1.0 / 120.0),
        )
        e = add(scaled(f1, b), scaled(f2, bb))
        unit = [[jnp.ones_like(p) if i == j else jnp.zeros_like(p) for j in range(3)] for i in range(3)]
        unit = jnp.stack([jnp.stack(r) for r in unit])
        e = e[0] + f0[0] * unit, e[1] + f0[1] * unit
        keep_b[k] = parts
        keep_bb[k] = join(bb)
        keep_e[k] = join(e)
        keep_s[k] = jnp.stack([p, s, h, f1[0], f1[1], f2[0], f2[1]])
        return carry

    lax.fori_loop(0, 2, block, 0)


def exponent_forces(links, staple_sum, force, keep_b, keep_bb, keep_e, keep_s, omega, direct):
    def block(k, carry):
        u, c, f = split(links[k]), split(staple_sum[k]), split(force[k])
        b, bb = skew_matrix(keep_b[k]), split(keep_bb[k])
        kept = keep_s[k]
        p, s, h = kept[0], kept[1], kept[2]
        f1, f2 = (kept[3], -kept[4]), (kept[5], -kept[6])
        d = mul_nd(f, u)

        def overlap(x):
            re = jnp.sum((d[0] * x[0] + d[1] * x[1]).reshape(9, 8, LANES), axis=0)
            im = jnp.sum((d[0] * x[1] - d[1] * x[0]).reshape(9, 8, LANES), axis=0)
            return re, im

        t0 = d[0][0, 0] + d[0][1, 1] + d[0][2, 2], -(d[1][0, 0] + d[1][1, 1] + d[1][2, 2])
        t1, t2 = overlap(b), overlap(bb)
        w0, w1, w2, w3, w4 = weights(h)
        pp, ps = p * p, p * s

        def slope(*changes):
            total = None
            for t, (re, im) in zip((t0, t1, t2), changes):
                term = t[0] * re - t[1] * im
                total = term if total is None else total + term
            return total

        gp = slope(
            (-s * h * (1.0 / 120.0), s * (1.0 / 120.0)),
            (w3[0] * (1.0 / 6.0) + p * (1.0 / 60.0), w3[1] * (1.0 / 6.0) + p * h * (1.0 / 60.0) + s * (1.0 / 360.0)),
            (w4[0] * (1.0 / 24.0) + p * (1.0 / 360.0), w4[1] * (1.0 / 24.0)),
        )
        gs = slope(
            (
                -w3[1] * (1.0 / 6.0) - p * h * (1.0 / 120.0) - s * (1.0 / 360.0),
                w3[0] * (1.0 / 6.0) + p * (1.0 / 120.0),
            ),
            (-w4[1] * (1.0 / 24.0), w4[0] * (1.0 / 24.0) + p * (1.0 / 360.0)),
            (-h * (1.0 / 120.0), jnp.full_like(h, 1.0 / 120.0)),
        )
        x0 = w1[0] - s * w4[1] * (1.0 / 6.0), w1[1] + s * w4[0] * (1.0 / 6.0) + ps * (1.0 / 120.0)
        x1 = (
            w2[0] + p * w4[0] * (1.0 / 6.0) - s * h * (1.0 / 24.0) + pp * (1.0 / 120.0),
            w2[1] + p * w4[1] * (1.0 / 6.0) + s * (1.0 / 24.0),
        )
        x2 = w3[0] * 0.5 + p * (1.0 / 24.0), w3[1] * 0.5 + p * h * (1.0 / 24.0) + s * (1.0 / 120.0)
        gh = slope(*[(-x[1], x[0]) for x in (x0, x1, x2)])
        d2 = scaled(f2, d)
        back = dagger(d2)
        half = 0.5 * (d2[0] + back[0]), 0.5 * (d2[1] + back[1])
        n = mul(b, half)
        d1 = scaled(f1, d)
        whole = (
            d1[0] - 2.0 * n[0] - gp * b[0] - gs * bb[1],
            d1[1] - 2.0 * n[1] - gp * b[1] + gs * bb[0],
        )
        parts = skew_parts(whole)
        shift = (gh - (parts[0] + parts[1] + parts[2])) * (1.0 / 3.0)
        parts = jnp.stack([WEIGHT * (v + shift) for v in parts[:3]] + [WEIGHT * v for v in parts[3:]])
        omega[k] = parts
        direct[k] = join(sub(mul_dn(split(keep_e[k]), f), mul(skew_matrix(parts), c)))
        return carry

    lax.fori_loop(0, 2, block, 0)


def kernel(counts, base_hbm, smeared_hbm, force_hbm, out_hbm, links, force, csum, direct, ga, gb, gc, gd, wa, wb, wc, wd,
           keep_t, keep_z, sa, sd, pa, pb, pc, pd, rim, keep_b, keep_bb, keep_e, keep_s, omega,
           send_u, recv_u, corner_u, send_w, recv_w, corner_w, in_sem, out_sem, send_sem, recv_sem):
    n_gz, n_ta = counts
    gz, ta = lax.axis_index("gz"), lax.axis_index("ta")
    zp, zm = lax.rem(gz + 1, n_gz), lax.rem(gz + n_gz - 1, n_gz)
    tp, tm = lax.rem(ta + 1, n_ta), lax.rem(ta + n_ta - 1, n_ta)
    where = ((zp, ta), (zm, ta), (gz, tp), (gz, tm), (zp, tm), (zm, tp))

    barrier = pltpu.get_barrier_semaphore()
    for device in where:
        pl.semaphore_signal(barrier, inc=1, device_id=device, device_id_type=MESH)

    def fetch(src, dst, slot):
        return [
            pltpu.make_async_copy(src.at[k], dst.at[k // 2, :, pl.ds(k % 2 * 4, 4)], in_sem.at[slot, k])
            for k in range(4)
        ]

    fetch_smeared = fetch(smeared_hbm, links.at[0], 0)
    fetch_base = fetch(base_hbm, links.at[1], 1)
    fetch_force = fetch(force_hbm, force, 2)
    for copy in fetch_smeared + fetch_base + fetch_force:
        copy.start()
    m = masks()

    def exchange(level, src, comps, send, recv, corner, slot):
        pack_sends(m, src[0], src[1], comps, send)
        moves = copies(src, send, recv, corner, send_sem.at[slot], recv_sem.at[slot], where)
        return moves

    for copy in fetch_smeared:
        copy.wait()
    moves_u0 = exchange(0, links.at[0], LINK, send_u.at[0], recv_u.at[0], corner_u.at[0], 0)
    pl.semaphore_wait(barrier, 6)
    for copy in moves_u0:
        copy.start()
    for copy in fetch_base:
        copy.wait()
    moves_u1 = exchange(1, links.at[1], LINK, send_u.at[1], recv_u.at[1], corner_u.at[1], 1)
    for copy in moves_u1:
        copy.start()
    for copy in fetch_force:
        copy.wait()

    def forward(level, moves):
        for copy in moves:
            copy.wait_recv()
        gather_into(m, links[level, 0], links[level, 1], recv_u.at[level], corner_u.at[level],
                    ga.at[level], gb.at[level], gc.at[level], gd.at[level])
        staples(ga.at[level], gb.at[level], gc.at[level], gd.at[level], keep_t.at[level], keep_z.at[level],
                sa.at[level], pb, pc, sd.at[level], rim)
        csum[level, 0], csum[level, 1] = scatter_sum(m, sa.at[level], pb, pc, sd.at[level], rim)
        exponent_parts(links.at[level], csum.at[level], keep_b.at[level], keep_bb.at[level], keep_e.at[level],
                       keep_s.at[level])

    def own_force(level):
        exponent_forces(links.at[level], csum.at[level], force, keep_b.at[level], keep_bb.at[level], keep_e.at[level],
                        keep_s.at[level], omega.at[level], direct)
        moves = exchange(level, omega.at[level], SKEW, send_w.at[level], recv_w.at[level], corner_w.at[level], 2 + level)
        for copy in moves:
            copy.start()
        return moves

    def finish(level, moves):
        for copy in moves:
            copy.wait_recv()
        gather_into(m, omega[level, 0], omega[level, 1], recv_w.at[level], corner_w.at[level], wa, wb, wc, wd)
        staple_forces(ga.at[level], gb.at[level], gc.at[level], gd.at[level], keep_t.at[level], keep_z.at[level],
                      sa.at[level], sd.at[level], wa, wb, wc, wd, pa, pb, pc, pd, rim)
        low, high = scatter_sum(m, pa, pb, pc, pd, rim)
        force[0] = low + direct[0]
        force[1] = high + direct[1]

    forward(0, moves_u0)
    moves_w0 = own_force(0)
    forward(1, moves_u1)
    finish(0, moves_w0)
    moves_w1 = own_force(1)
    finish(1, moves_w1)
    stores = [
        pltpu.make_async_copy(force.at[k // 2, :, pl.ds(k % 2 * 4, 4)], out_hbm.at[k], out_sem.at[k]) for k in range(4)
    ]
    for copy in stores:
        copy.start()
    for copy in moves_u0 + moves_u1 + moves_w0 + moves_w1:
        copy.wait_send()
    for copy in stores:
        copy.wait()


def solution(mesh):
    counts = (mesh.shape["gz"], mesh.shape["ta"])

    def vmem(*shape):
        return pltpu.VMEM(shape + (8, LANES), jnp.float32)

    def per_device(base_links, smeared_links, top_force):
        def flat(v):
            return v.reshape(4, LINK, 4, LANES)

        out = pl.pallas_call(
            lambda *refs: kernel(counts, *refs),
            out_shape=jax.ShapeDtypeStruct((4, LINK, 4, LANES), jnp.float32),
            in_specs=[pl.BlockSpec(memory_space=pl.ANY)] * 3,
            out_specs=pl.BlockSpec(memory_space=pl.ANY),
            scratch_shapes=[
                vmem(2, 2, LINK),
                vmem(2, LINK),
                vmem(2, 2, LINK),
                vmem(2, LINK),
                vmem(2, 5, LINK),
                vmem(2, 5, LINK),
                vmem(2, 3, LINK),
                vmem(2, 5, LINK),
                vmem(5, SKEW),
                vmem(5, SKEW),
                vmem(3, SKEW),
                vmem(5, SKEW),
                vmem(2, 5, LINK),
                vmem(2, 3, LINK),
                vmem(2, 3, LINK),
                vmem(2, 3, LINK),
                vmem(3, LINK),
                vmem(3, LINK),
                vmem(3, LINK),
                vmem(3, LINK),
                vmem(2, LINK),
                vmem(2, 2, SKEW),
                vmem(2, 2, LINK),
                vmem(2, 2, LINK),
                vmem(2, 2, 7),
                vmem(2, 2, SKEW),
                vmem(2, 4, LINK),
                vmem(2, 4, LINK),
                vmem(2, LINK),
                vmem(2, 4, SKEW),
                vmem(2, 4, SKEW),
                vmem(2, SKEW),
                pltpu.SemaphoreType.DMA((3, 4)),
                pltpu.SemaphoreType.DMA((4,)),
                pltpu.SemaphoreType.DMA((4, 6)),
                pltpu.SemaphoreType.DMA((4, 6)),
            ],
            compiler_params=pltpu.CompilerParams(
                collective_id=0, has_side_effects=True, vmem_limit_bytes=48 * 1024 * 1024
            ),
            name="stout_back",
        )(flat(base_links), flat(smeared_links), flat(top_force))
        return out.reshape(base_links.shape)

    spec = P(None, None, None, None, "gz", "ta", None)
    return jax.shard_map(per_device, mesh=mesh, in_specs=(spec, spec, spec), out_specs=spec, check_vma=False)
```

```python
import jax
import jax.numpy as jnp
from jax import lax
from jax.experimental import pallas as pl
from jax.experimental.pallas import tpu as pltpu
from jax.sharding import PartitionSpec as P

MESH = pl.DeviceIdType.MESH
LY = 8
WEIGHT = 0.1
LANES = 128
LINK = 18
SKEW = 9


def masks():
    row = lax.broadcasted_iota(jnp.int32, (1, 8, LANES), 1)
    col = lax.broadcasted_iota(jnp.int32, (1, 8, LANES), 2) % LY
    return {
        "low": row < 4,
        "even": row % 2 == 0,
        "near": row % 4 < 2,
        "row": row,
        "first": col == 0,
        "last": col == LY - 1,
    }


def pick(mask, yes, no):
    return jnp.where(jnp.broadcast_to(mask, yes.shape), yes, no)


def rows(v, shift):
    return pltpu.roll(v, shift % 8, 1)


def fwd_x(v):
    return pltpu.roll(v, LANES - LY, 2)


def back_x(v):
    return pltpu.roll(v, LY, 2)


def fwd_y(m, v):
    return pick(m["last"], pltpu.roll(v, LY - 1, 2), pltpu.roll(v, LANES - 1, 2))


def back_y(m, v):
    return pick(m["first"], pltpu.roll(v, LANES - LY + 1, 2), pltpu.roll(v, 1, 2))


def fwd_xy(m, v):
    return pick(m["low"], fwd_x(v), fwd_y(m, v))


def back_xy(m, v):
    return pick(m["low"], back_x(v), back_y(m, v))


def split(v):
    return v[:9].reshape(3, 3, 8, LANES), v[9:].reshape(3, 3, 8, LANES)


def join(m):
    return jnp.concatenate([m[0].reshape(9, 8, LANES), m[1].reshape(9, 8, LANES)], axis=0)


def outer_sum(lefts, rights):
    total = None
    for left, right in zip(lefts, rights):
        term = left[:, None] * right[None, :]
        total = term if total is None else total + term
    return total


def columns(a):
    return [a[:, k] for k in range(3)]


def lines(a):
    return [a[k] for k in range(3)]


def product(left, right, sl, sr):
    (ar, ai), (br, bi) = left, right
    rr, ii = outer_sum(ar, br), outer_sum(ai, bi)
    ri, ir = outer_sum(ar, bi), outer_sum(ai, br)
    re = rr - ii if sl * sr > 0 else rr + ii
    if sl > 0 and sr > 0:
        im = ri + ir
    elif sl < 0 and sr > 0:
        im = ri - ir
    else:
        im = ir - ri
    return re, im


def mul(a, b):
    return product((columns(a[0]), columns(a[1])), (lines(b[0]), lines(b[1])), 1, 1)


def mul_dn(a, b):
    return product((lines(a[0]), lines(a[1])), (lines(b[0]), lines(b[1])), -1, 1)


def mul_nd(a, b):
    return product((columns(a[0]), columns(a[1])), (columns(b[0]), columns(b[1])), 1, -1)


def add(a, b):
    return a[0] + b[0], a[1] + b[1]


def sub(a, b):
    return a[0] - b[0], a[1] - b[1]


def flip(v):
    return jnp.stack([v[:, 0], v[:, 1], v[:, 2]], axis=0)


def dagger(a):
    return flip(a[0]), -flip(a[1])


def scaled(c, a):
    cr, ci = c
    return cr * a[0] - ci * a[1], cr * a[1] + ci * a[0]


def skew_parts(a):
    re, im = a
    out = [im[0, 0], im[1, 1], im[2, 2]]
    for i, j in ((0, 1), (0, 2), (1, 2)):
        out += [0.5 * (re[i, j] - re[j, i]), 0.5 * (im[i, j] + im[j, i])]
    return out


def skew_matrix(v):
    d0, d1, d2, r01, i01, r02, i02, r12, i12 = [v[k] for k in range(9)]
    zero = jnp.zeros_like(d0)
    re = jnp.stack([jnp.stack([zero, r01, r02]), jnp.stack([-r01, zero, r12]), jnp.stack([-r02, -r12, zero])])
    im = jnp.stack([jnp.stack([d0, i01, i02]), jnp.stack([i01, d1, i12]), jnp.stack([i02, i12, d2])])
    return re, im


def pack_sends(m, low, high, comps, send):
    send[0, :comps] = pick(m["near"], rows(low, -2), high)
    send[1, :comps] = pick(m["near"], high, rows(low, 2))
    send[2, :comps] = pick(m["even"], rows(low, -1), high)
    send[3, :comps] = pick(m["even"], rows(high, 4), rows(low, 1))


def remote(src, dst, sems, k, device):
    return pltpu.make_async_remote_copy(
        src_ref=src, dst_ref=dst, send_sem=sems[0].at[k], recv_sem=sems[1].at[k], device_id=device, device_id_type=MESH
    )


def link_copies(src, recv, corner, sems, where):
    ahead, behind = [], []
    k = 0

    def put(out, direction, row, count, slot, to):
        nonlocal k
        dst = corner if slot > 3 else recv.at[slot]
        out.append(
            remote(src.at[direction, :, pl.ds(row, count)], dst.at[:, pl.ds(to, count)], sems, k, where[slot])
        )
        k += 1

    put(behind, 2, 2, 1, 4, 1)
    put(behind, 3, 1, 1, 5, 3)
    for direction, to in ((0, 2), (1, 6), (3, 4)):
        put(ahead, direction, 0, 2, 1, to)
    for direction, to in ((0, 1), (1, 5), (2, 4)):
        put(ahead, direction, 0, 1, 3, to)
        put(ahead, direction, 2, 1, 3, to + 2)
    for direction, to in ((0, 0), (2, 2), (1, 4), (3, 6)):
        put(behind, direction, 2, 2, 0, to)
    for direction, to in ((0, 0), (2, 1), (1, 4), (3, 5)):
        put(behind, direction, 1, 1, 2, to)
        put(behind, direction, 3, 1, 2, to + 2)
    return ahead, behind


def term_copies(src, send, recv, corner, sems, where):
    behind = [
        remote(src.at[1, :, pl.ds(2, 1)], corner.at[:, pl.ds(1, 1)], sems, 4, where[4]),
        remote(src.at[1, :, pl.ds(5, 1)], corner.at[:, pl.ds(3, 1)], sems, 5, where[5]),
        remote(send.at[0], recv.at[0], sems, 0, where[0]),
        remote(send.at[2], recv.at[2], sems, 2, where[2]),
    ]
    ahead = [
        remote(send.at[1, :, pl.ds(2, 6)], recv.at[1, :, pl.ds(2, 6)], sems, 1, where[1]),
        remote(send.at[3, :, pl.ds(1, 7)], recv.at[3, :, pl.ds(1, 7)], sems, 3, where[3]),
    ]
    return ahead, behind


def start(moves):
    ahead, behind = moves
    for copy in behind[:2] + ahead + behind[2:]:
        copy.start()


def gather_own(m, low, high, ga, gb, gd):
    ga[0], gd[0] = pick(m["low"], low, rows(high, 4)), pick(m["low"], rows(low, 4), high)
    ga[1], gd[1] = low, high
    gb[1] = fwd_xy(m, high)
    d2 = rows(high, 4)
    ga[2], gd[2] = low, d2
    gb[2] = fwd_xy(m, d2)


def gather_ahead(m, recv, ga, gb, gc, gd):
    at_zp, at_tp = recv[1], recv[3]
    a0, d0, low = ga[0], gd[0], ga[1]
    gb[0] = pick(m["low"], fwd_x(d0), pick(m["near"], rows(d0, -2), rows(at_zp, 2)))
    gc[0] = pick(m["low"], fwd_y(m, a0), pick(m["even"], rows(a0, -1), rows(at_tp, 1)))
    up_z = pick(m["near"], rows(low, -2), at_zp)
    up_t = pick(m["even"], rows(low, -1), at_tp)
    gc[1] = pick(m["low"], up_z, up_t)
    gc[2] = pick(m["low"], up_t, up_z)


def gather_behind(m, recv, corner, ga, gb, gd):
    at_zm, at_tm = recv[0], recv[2]
    diag = corner[...]
    row = m["row"]
    dz = pick(row < 2, rows(at_zm, -2), pick(row < 4, at_zm, pick(row < 6, rows(at_zm, 2), rows(at_zm, 4))))
    ga[3], gd[3] = at_zm, dz
    gb[3] = pick(row < 6, fwd_xy(m, dz), pick(m["even"], rows(at_zm, 3), rows(diag, 6)))
    dt = pick(m["low"], pick(m["even"], rows(at_tm, 3), rows(at_tm, 4)), pick(m["even"], rows(at_tm, -1), at_tm))
    ga[4], gd[4] = at_tm, dt
    gb[4] = pick(m["even"], fwd_xy(m, dt), pick(row < 2, rows(at_tm, 2), diag))


def scatter_sum(m, pa, pb, pc, pd, rim):
    a0, b0, c0, d0 = pa[0], pb[0], pc[0], pd[0]
    a1, b1, c1, d1 = pa[1], pb[1], pc[1], pd[1]
    a2, b2, c2, d2 = pa[2], pb[2], pc[2], pd[2]
    rz, rt = rim[0], rim[1]
    from_z = pick(m["near"], rz, rows(pick(m["low"], c1, c2), 2))
    from_t = pick(m["even"], rt, rows(pick(m["low"], c2, c1), 1))
    low = (a1 + a2) + (from_z + from_t)
    low = low + pick(m["low"], a0 + back_y(m, c0), rows(d0 + back_x(b0), 4))
    high = (d1 + back_xy(m, b1)) + rows(d2 + back_xy(m, b2), 4)
    z_part = a0 + pick(m["even"], rows(rt, 3), rows(c0, 1))
    t_part = d0 + pick(m["near"], rows(rz, -2), rows(b0, 2))
    high = high + pick(m["low"], rows(z_part, 4), t_part)
    return low, high


def each(first, last, body):
    def step(k, carry):
        body(k)
        return carry

    lax.fori_loop(first, last, step, 0)


def staples_own(ga, gb, gd, keep_t, pc):
    def corner_products(k):
        keep_t[k] = join(mul_dn(split(ga[k]), split(gd[k])))

    def ends(k):
        pc[k] = join(mul_dn(split(keep_t[k]), split(gb[k])))

    each(0, 3, corner_products)
    each(1, 3, ends)


def staples_ahead(ga, gb, gc, gd, keep_t, keep_z, pa, pb, pc, pd):
    pc[0] = join(mul_dn(split(keep_t[0]), split(gb[0])))

    def block(k):
        c = split(gc[k])
        pb[k] = join(mul(split(keep_t[k]), c))
        z = mul_nd(c, split(gb[k]))
        keep_z[k] = join(z)
        pa[k] = join(mul(split(gd[k]), z))
        pd[k] = join(mul_nd(split(ga[k]), z))

    each(0, 3, block)


def staples_behind(ga, gb, gd, keep_t, rim):
    def block(k):
        t = mul_dn(split(ga[k]), split(gd[k]))
        keep_t[k] = join(t)
        rim[k - 3] = join(mul_dn(t, split(gb[k])))

    each(3, 5, block)


def forces_own(ga, gb, gd, keep_t, keep_z, sa, sd, wa, wb, wd, keep_n, zb, pa, pc, pd):
    def block(k):
        va, vd = wa[k], wd[k]
        keep_n[k] = join(mul_dn(split(ga[k]), mul(skew_matrix(va - vd), split(gd[k]))))
        pa[k] = join(mul(skew_matrix(vd), split(sa[k])))
        pd[k] = join(mul(skew_matrix(va), split(sd[k])))

    each(0, 3, block)
    each(1, 3, lambda k: force_end(gb, keep_t, keep_z, wb, keep_n, zb, pc, k))


def force_end(gb, keep_t, keep_z, wb, keep_n, zb, pc, k):
    ob = skew_matrix(wb[k])
    pc[k] = join(mul(sub(mul_dn(split(keep_t[k]), ob), dagger(split(keep_n[k]))), split(gb[k])))
    zb[k] = join(mul(split(keep_z[k]), ob))


def forces_ahead(ga, gb, gc, gd, keep_t, keep_z, wb, wc, keep_n, zb, pa, pb, pc, pd):
    force_end(gb, keep_t, keep_z, wb, keep_n, zb, pc, 0)

    def block(k):
        oc = skew_matrix(wc[k])
        pb[k] = join(mul(sub(mul(split(keep_t[k]), oc), split(keep_n[k])), split(gc[k])))
        q = sub(mul(oc, split(keep_z[k])), split(zb[k]))
        pa[k] = join(add(mul(split(gd[k]), q), split(pa[k])))
        pd[k] = join(add(mul_nd(split(ga[k]), q), split(pd[k])))

    each(0, 3, block)


def forces_behind(ga, gb, gd, keep_t, wa, wb, wd, rim):
    def block(k):
        n = mul_dn(split(ga[k]), mul(skew_matrix(wa[k] - wd[k]), split(gd[k])))
        t = split(keep_t[k])
        rim[k - 3] = join(mul(sub(mul_dn(t, skew_matrix(wb[k])), dagger(n)), split(gb[k])))

    each(3, 5, block)


def weights(h):
    hh = h * h
    r2 = 1.0 - hh * 0.5
    r4 = r2 + hh * hh * (1.0 / 24.0)
    r6 = r4 - hh * hh * hh * (1.0 / 720.0)
    i3 = h - h * hh * (1.0 / 6.0)
    i5 = i3 + h * hh * hh * (1.0 / 120.0)
    return (r6, i5), (r4, i5), (r4, i3), (r2, i3), (r2, h)


def exponent_parts(links, staple_sum, keep_b, keep_bb, keep_e, keep_s):
    def block(k, carry):
        u, c = split(links[k]), split(staple_sum[k])
        omega = mul_nd(c, u)
        parts = [WEIGHT * v for v in skew_parts(omega)]
        h = (parts[0] + parts[1] + parts[2]) * (1.0 / 3.0)
        parts = jnp.stack([v - h for v in parts[:3]] + parts[3:])
        b = skew_matrix(parts)
        bb = mul(b, b)
        p = 0.5 * (bb[0][0, 0] + bb[0][1, 1] + bb[0][2, 2])
        s = jnp.sum((b[1] * bb[0] - b[0] * bb[1]).reshape(9, 8, LANES), axis=0) * (1.0 / 3.0)
        w0, w1, w2, w3, w4 = weights(h)
        pp, ps = p * p, p * s
        f0 = (
            w0[0] - s * w3[1] * (1.0 / 6.0) - ps * h * (1.0 / 120.0) - s * s * (1.0 / 720.0),
            w0[1] + s * w3[0] * (1.0 / 6.0) + ps * (1.0 / 120.0),
        )
        f1 = (
            w1[0] + p * w3[0] * (1.0 / 6.0) - s * w4[1] * (1.0 / 24.0) + pp * (1.0 / 120.0),
            w1[1] + p * w3[1] * (1.0 / 6.0) + s * w4[0] * (1.0 / 24.0) + pp * h * (1.0 / 120.0) + ps * (1.0 / 360.0),
        )
        f2 = (
            w2[0] * 0.5 + p * w4[0] * (1.0 / 24.0) - s * h * (1.0 / 120.0) + pp * (1.0 / 720.0),
            w2[1] * 0.5 + p * w4[1] * (1.0 / 24.0) + s * (1.0 / 120.0),
        )
        e = add(scaled(f1, b), scaled(f2, bb))
        unit = [[jnp.ones_like(p) if i == j else jnp.zeros_like(p) for j in range(3)] for i in range(3)]
        unit = jnp.stack([jnp.stack(r) for r in unit])
        e = e[0] + f0[0] * unit, e[1] + f0[1] * unit
        keep_b[k] = parts
        keep_bb[k] = join(bb)
        keep_e[k] = join(e)
        keep_s[k] = jnp.stack([p, s, h, f1[0], f1[1], f2[0], f2[1]])
        return carry

    lax.fori_loop(0, 2, block, 0)


def exponent_forces(links, force, keep_b, keep_bb, keep_s, omega):
    def block(k, carry):
        u, f = split(links[k]), split(force[k])
        b, bb = skew_matrix(keep_b[k]), split(keep_bb[k])
        kept = keep_s[k]
        p, s, h = kept[0], kept[1], kept[2]
        f1, f2 = (kept[3], -kept[4]), (kept[5], -kept[6])
        d = mul_nd(f, u)

        def overlap(x):
            re = jnp.sum((d[0] * x[0] + d[1] * x[1]).reshape(9, 8, LANES), axis=0)
            im = jnp.sum((d[0] * x[1] - d[1] * x[0]).reshape(9, 8, LANES), axis=0)
            return re, im

        t0 = d[0][0, 0] + d[0][1, 1] + d[0][2, 2], -(d[1][0, 0] + d[1][1, 1] + d[1][2, 2])
        t1, t2 = overlap(b), overlap(bb)
        w0, w1, w2, w3, w4 = weights(h)
        pp, ps = p * p, p * s

        def slope(*changes):
            total = None
            for t, (re, im) in zip((t0, t1, t2), changes):
                term = t[0] * re - t[1] * im
                total = term if total is None else total + term
            return total

        gp = slope(
            (-s * h * (1.0 / 120.0), s * (1.0 / 120.0)),
            (w3[0] * (1.0 / 6.0) + p * (1.0 / 60.0), w3[1] * (1.0 / 6.0) + p * h * (1.0 / 60.0) + s * (1.0 / 360.0)),
            (w4[0] * (1.0 / 24.0) + p * (1.0 / 360.0), w4[1] * (1.0 / 24.0)),
        )
        gs = slope(
            (
                -w3[1] * (1.0 / 6.0) - p * h * (1.0 / 120.0) - s * (1.0 / 360.0),
                w3[0] * (1.0 / 6.0) + p * (1.0 / 120.0),
            ),
            (-w4[1] * (1.0 / 24.0), w4[0] * (1.0 / 24.0) + p * (1.0 / 360.0)),
            (-h * (1.0 / 120.0), jnp.full_like(h, 1.0 / 120.0)),
        )
        x0 = w1[0] - s * w4[1] * (1.0 / 6.0), w1[1] + s * w4[0] * (1.0 / 6.0) + ps * (1.0 / 120.0)
        x1 = (
            w2[0] + p * w4[0] * (1.0 / 6.0) - s * h * (1.0 / 24.0) + pp * (1.0 / 120.0),
            w2[1] + p * w4[1] * (1.0 / 6.0) + s * (1.0 / 24.0),
        )
        x2 = w3[0] * 0.5 + p * (1.0 / 24.0), w3[1] * 0.5 + p * h * (1.0 / 24.0) + s * (1.0 / 120.0)
        gh = slope(*[(-x[1], x[0]) for x in (x0, x1, x2)])
        d2 = scaled(f2, d)
        back = dagger(d2)
        half = 0.5 * (d2[0] + back[0]), 0.5 * (d2[1] + back[1])
        n = mul(b, half)
        d1 = scaled(f1, d)
        whole = (
            d1[0] - 2.0 * n[0] - gp * b[0] - gs * bb[1],
            d1[1] - 2.0 * n[1] - gp * b[1] + gs * bb[0],
        )
        parts = skew_parts(whole)
        shift = (gh - (parts[0] + parts[1] + parts[2])) * (1.0 / 3.0)
        parts = jnp.stack([WEIGHT * (v + shift) for v in parts[:3]] + [WEIGHT * v for v in parts[3:]])
        omega[k] = parts
        return carry

    lax.fori_loop(0, 2, block, 0)


def direct_forces(staple_sum, force, keep_e, omega, direct):
    def block(k):
        own = mul_dn(split(keep_e[k]), split(force[k]))
        direct[k] = join(sub(own, mul(skew_matrix(omega[k]), split(staple_sum[k]))))

    each(0, 2, block)


def kernel(counts, base_hbm, smeared_hbm, force_hbm, out_hbm, links, force, csum, direct, ga, gb, gc, gd, wa, wb, wc, wd,
           keep_t, keep_z, sa, sd, keep_n, zb, pa, pb, pc, pd, rim, keep_b, keep_bb, keep_e, keep_s, omega,
           recv_u, corner_u, send_w, recv_w, corner_w, in_sem, out_sem, send_u_sem, recv_u_sem, send_w_sem, recv_w_sem):
    n_gz, n_ta = counts
    gz, ta = lax.axis_index("gz"), lax.axis_index("ta")
    zp, zm = lax.rem(gz + 1, n_gz), lax.rem(gz + n_gz - 1, n_gz)
    tp, tm = lax.rem(ta + 1, n_ta), lax.rem(ta + n_ta - 1, n_ta)
    where = ((zp, ta), (zm, ta), (gz, tp), (gz, tm), (zp, tm), (zm, tp))

    barrier = pltpu.get_barrier_semaphore()
    for device in where:
        pl.semaphore_signal(barrier, inc=1, device_id=device, device_id_type=MESH)

    def fetch(src, dst, slot):
        return [
            pltpu.make_async_copy(src.at[k], dst.at[k // 2, :, pl.ds(k % 2 * 4, 4)], in_sem.at[slot, k])
            for k in range(4)
        ]

    fetches = fetch(smeared_hbm, links.at[0], 0) + fetch(base_hbm, links.at[1], 1) + fetch(force_hbm, force, 2)
    for copy in fetches:
        copy.start()
    m = masks()
    moves_u = [
        link_copies(
            src, recv_u.at[level], corner_u.at[level], (send_u_sem.at[level], recv_u_sem.at[level]), where
        )
        for level, src in ((0, smeared_hbm), (1, base_hbm))
    ]
    pl.semaphore_wait(barrier, 6)
    for moves in moves_u:
        start(moves)
    for copy in fetches:
        copy.wait()

    def of(level, *refs):
        return [r.at[level] for r in refs]

    def landed(copies):
        for copy in copies:
            copy.wait_recv()

    def before(level):
        la, lb, ld, lt = of(level, ga, gb, gd, keep_t)
        gather_own(m, links[level, 0], links[level, 1], la, lb, ld)
        staples_own(la, lb, ld, lt, pc.at[level])

    def forward(level):
        la, lb, lc, ld, lt, lz = of(level, ga, gb, gc, gd, keep_t, keep_z)
        ahead, behind = moves_u[level]
        landed(ahead)
        gather_ahead(m, recv_u.at[level], la, lb, lc, ld)
        staples_ahead(la, lb, lc, ld, lt, lz, sa.at[level], pb, pc.at[level], sd.at[level])
        landed(behind)
        gather_behind(m, recv_u.at[level], corner_u.at[level], la, lb, ld)
        staples_behind(la, lb, ld, lt, rim)
        csum[level, 0], csum[level, 1] = scatter_sum(m, sa.at[level], pb, pc.at[level], sd.at[level], rim)
        exponent_parts(links.at[level], csum.at[level], *of(level, keep_b, keep_bb, keep_e, keep_s))

    def send_force(level):
        exponent_forces(links.at[level], force, *of(level, keep_b, keep_bb, keep_s, omega))
        pack_sends(m, omega[level, 0], omega[level, 1], SKEW, send_w.at[level])
        moves = term_copies(
            omega.at[level], send_w.at[level], recv_w.at[level], corner_w.at[level],
            (send_w_sem.at[level], recv_w_sem.at[level]), where,
        )
        start(moves)
        return moves

    def finish(level, moves, meanwhile):
        la, lb, lc, ld, lt, lz = of(level, ga, gb, gc, gd, keep_t, keep_z)
        direct_forces(csum.at[level], force, keep_e.at[level], omega.at[level], direct)
        gather_own(m, omega[level, 0], omega[level, 1], wa, wb, wd)
        forces_own(la, lb, ld, lt, lz, sa.at[level], sd.at[level], wa, wb, wd, keep_n, zb, pa, pc.at[level], pd)
        meanwhile()
        ahead, behind = moves
        landed(ahead)
        gather_ahead(m, recv_w.at[level], wa, wb, wc, wd)
        forces_ahead(la, lb, lc, ld, lt, lz, wb, wc, keep_n, zb, pa, pb, pc.at[level], pd)
        landed(behind)
        gather_behind(m, recv_w.at[level], corner_w.at[level], wa, wb, wd)
        forces_behind(la, lb, ld, lt, wa, wb, wd, rim)
        low, high = scatter_sum(m, pa, pb, pc.at[level], pd, rim)
        force[0] = low + direct[0]
        force[1] = high + direct[1]

    before(0)
    before(1)
    forward(0)
    moves_w0 = send_force(0)
    finish(0, moves_w0, lambda: forward(1))
    moves_w1 = send_force(1)
    finish(1, moves_w1, lambda: None)
    stores = [
        pltpu.make_async_copy(force.at[k // 2, :, pl.ds(k % 2 * 4, 4)], out_hbm.at[k], out_sem.at[k]) for k in range(4)
    ]
    for copy in stores:
        copy.start()
    for ahead, behind in (*moves_u, moves_w0, moves_w1):
        for copy in ahead + behind:
            copy.wait_send()
    for copy in stores:
        copy.wait()


def solution(mesh):
    counts = (mesh.shape["gz"], mesh.shape["ta"])

    def vmem(*shape):
        return pltpu.VMEM(shape + (8, LANES), jnp.float32)

    def per_device(base_links, smeared_links, top_force):
        def flat(v):
            return v.reshape(4, LINK, 4, LANES)

        out = pl.pallas_call(
            lambda *refs: kernel(counts, *refs),
            out_shape=jax.ShapeDtypeStruct((4, LINK, 4, LANES), jnp.float32),
            in_specs=[pl.BlockSpec(memory_space=pl.ANY)] * 3,
            out_specs=pl.BlockSpec(memory_space=pl.ANY),
            scratch_shapes=[
                vmem(2, 2, LINK),
                vmem(2, LINK),
                vmem(2, 2, LINK),
                vmem(2, LINK),
                vmem(2, 5, LINK),
                vmem(2, 5, LINK),
                vmem(2, 3, LINK),
                vmem(2, 5, LINK),
                vmem(5, SKEW),
                vmem(5, SKEW),
                vmem(3, SKEW),
                vmem(5, SKEW),
                vmem(2, 5, LINK),
                vmem(2, 3, LINK),
                vmem(2, 3, LINK),
                vmem(2, 3, LINK),
                vmem(3, LINK),
                vmem(3, LINK),
                vmem(3, LINK),
                vmem(3, LINK),
                vmem(2, 3, LINK),
                vmem(3, LINK),
                vmem(2, LINK),
                vmem(2, 2, SKEW),
                vmem(2, 2, LINK),
                vmem(2, 2, LINK),
                vmem(2, 2, 7),
                vmem(2, 2, SKEW),
                vmem(2, 4, LINK),
                vmem(2, LINK),
                vmem(2, 4, SKEW),
                vmem(2, 4, SKEW),
                vmem(2, SKEW),
                pltpu.SemaphoreType.DMA((3, 4)),
                pltpu.SemaphoreType.DMA((4,)),
                pltpu.SemaphoreType.DMA((2, 23)),
                pltpu.SemaphoreType.DMA((2, 23)),
                pltpu.SemaphoreType.DMA((2, 6)),
                pltpu.SemaphoreType.DMA((2, 6)),
            ],
            compiler_params=pltpu.CompilerParams(
                collective_id=0, has_side_effects=True, vmem_limit_bytes=67_043_328
            ),
            name="stout_back",
        )(flat(base_links), flat(smeared_links), flat(top_force))
        return out.reshape(base_links.shape)

    spec = P(None, None, None, None, "gz", "ta", None)
    return jax.shard_map(per_device, mesh=mesh, in_specs=(spec, spec, spec), out_specs=spec, check_vma=False)
```

```python
import jax
import jax.numpy as jnp
from jax import lax
from jax.experimental import pallas as pl
from jax.experimental.pallas import tpu as pltpu
from jax.sharding import PartitionSpec as P

MESH = pl.DeviceIdType.MESH
LY = 8
WEIGHT = 0.1
LANES = 128
LINK = 18
SKEW = 9


def masks():
    row = lax.broadcasted_iota(jnp.int32, (1, 8, LANES), 1)
    col = lax.broadcasted_iota(jnp.int32, (1, 8, LANES), 2) % LY
    return {
        "low": row < 4,
        "even": row % 2 == 0,
        "near": row % 4 < 2,
        "row": row,
        "first": col == 0,
        "last": col == LY - 1,
    }


def pick(mask, yes, no):
    return jnp.where(jnp.broadcast_to(mask, yes.shape), yes, no)


def rows(v, shift):
    return pltpu.roll(v, shift % 8, 1)


def fwd_x(v):
    return pltpu.roll(v, LANES - LY, 2)


def back_x(v):
    return pltpu.roll(v, LY, 2)


def fwd_y(m, v):
    return pick(m["last"], pltpu.roll(v, LY - 1, 2), pltpu.roll(v, LANES - 1, 2))


def back_y(m, v):
    return pick(m["first"], pltpu.roll(v, LANES - LY + 1, 2), pltpu.roll(v, 1, 2))


def fwd_xy(m, v):
    return pick(m["low"], fwd_x(v), fwd_y(m, v))


def back_xy(m, v):
    return pick(m["low"], back_x(v), back_y(m, v))


def split(v):
    return v[:9].reshape(3, 3, 8, LANES), v[9:].reshape(3, 3, 8, LANES)


def join(m):
    return jnp.concatenate([m[0].reshape(9, 8, LANES), m[1].reshape(9, 8, LANES)], axis=0)


def outer_sum(lefts, rights):
    total = None
    for left, right in zip(lefts, rights):
        term = left[:, None] * right[None, :]
        total = term if total is None else total + term
    return total


def columns(a):
    return [a[:, k] for k in range(3)]


def lines(a):
    return [a[k] for k in range(3)]


def product(left, right, sl, sr):
    (ar, ai), (br, bi) = left, right
    rr, ii = outer_sum(ar, br), outer_sum(ai, bi)
    ri, ir = outer_sum(ar, bi), outer_sum(ai, br)
    re = rr - ii if sl * sr > 0 else rr + ii
    if sl > 0 and sr > 0:
        im = ri + ir
    elif sl < 0 and sr > 0:
        im = ri - ir
    else:
        im = ir - ri
    return re, im


def mul(a, b):
    return product((columns(a[0]), columns(a[1])), (lines(b[0]), lines(b[1])), 1, 1)


def mul_dn(a, b):
    return product((lines(a[0]), lines(a[1])), (lines(b[0]), lines(b[1])), -1, 1)


def mul_nd(a, b):
    return product((columns(a[0]), columns(a[1])), (columns(b[0]), columns(b[1])), 1, -1)


def add(a, b):
    return a[0] + b[0], a[1] + b[1]


def sub(a, b):
    return a[0] - b[0], a[1] - b[1]


def flip(v):
    return jnp.stack([v[:, 0], v[:, 1], v[:, 2]], axis=0)


def dagger(a):
    return flip(a[0]), -flip(a[1])


def scaled(c, a):
    cr, ci = c
    return cr * a[0] - ci * a[1], cr * a[1] + ci * a[0]


def skew_parts(a):
    re, im = a
    out = [im[0, 0], im[1, 1], im[2, 2]]
    for i, j in ((0, 1), (0, 2), (1, 2)):
        out += [0.5 * (re[i, j] - re[j, i]), 0.5 * (im[i, j] + im[j, i])]
    return out


def skew_matrix(v):
    d0, d1, d2, r01, i01, r02, i02, r12, i12 = [v[k] for k in range(9)]
    zero = jnp.zeros_like(d0)
    re = jnp.stack([jnp.stack([zero, r01, r02]), jnp.stack([-r01, zero, r12]), jnp.stack([-r02, -r12, zero])])
    im = jnp.stack([jnp.stack([d0, i01, i02]), jnp.stack([i01, d1, i12]), jnp.stack([i02, i12, d2])])
    return re, im


def pack_sends(m, low, high, comps, send):
    send[0, :comps] = pick(m["near"], rows(low, -2), high)
    send[1, :comps] = pick(m["near"], high, rows(low, 2))
    send[2, :comps] = pick(m["even"], rows(low, -1), high)
    send[3, :comps] = pick(m["even"], rows(high, 4), rows(low, 1))


def remote(src, dst, sems, k, device):
    return pltpu.make_async_remote_copy(
        src_ref=src, dst_ref=dst, send_sem=sems[0].at[k], recv_sem=sems[1].at[k], device_id=device, device_id_type=MESH
    )


def link_copies(src, recv, corner, sems, where):
    ahead, behind = [], []
    k = 0

    def put(out, direction, row, count, slot, to):
        nonlocal k
        dst = corner if slot > 3 else recv.at[slot]
        out.append(
            remote(src.at[direction, :, pl.ds(row, count)], dst.at[:, pl.ds(to, count)], sems, k, where[slot])
        )
        k += 1

    put(behind, 2, 2, 1, 4, 1)
    put(behind, 3, 1, 1, 5, 3)
    for direction, to in ((0, 2), (1, 6), (3, 4)):
        put(ahead, direction, 0, 2, 1, to)
    for direction, to in ((0, 1), (1, 5), (2, 4)):
        put(ahead, direction, 0, 1, 3, to)
        put(ahead, direction, 2, 1, 3, to + 2)
    for direction, to in ((0, 0), (2, 2), (1, 4), (3, 6)):
        put(behind, direction, 2, 2, 0, to)
    for direction, to in ((0, 0), (2, 1), (1, 4), (3, 5)):
        put(behind, direction, 1, 1, 2, to)
        put(behind, direction, 3, 1, 2, to + 2)
    return ahead, behind


def term_copies(src, send, recv, corner, sems, where):
    behind = [
        remote(src.at[1, :, pl.ds(2, 1)], corner.at[:, pl.ds(1, 1)], sems, 4, where[4]),
        remote(src.at[1, :, pl.ds(5, 1)], corner.at[:, pl.ds(3, 1)], sems, 5, where[5]),
        remote(send.at[0], recv.at[0], sems, 0, where[0]),
        remote(send.at[2], recv.at[2], sems, 2, where[2]),
    ]
    ahead = [
        remote(send.at[1, :, pl.ds(2, 6)], recv.at[1, :, pl.ds(2, 6)], sems, 1, where[1]),
        remote(send.at[3, :, pl.ds(1, 7)], recv.at[3, :, pl.ds(1, 7)], sems, 3, where[3]),
    ]
    return ahead, behind


def start(moves):
    ahead, behind = moves
    for copy in behind[:2] + ahead + behind[2:]:
        copy.start()


def gather_own(m, low, high, ga, gb, gd):
    ga[0], gd[0] = pick(m["low"], low, rows(high, 4)), pick(m["low"], rows(low, 4), high)
    ga[1], gd[1] = low, high
    gb[1] = fwd_xy(m, high)
    d2 = rows(high, 4)
    ga[2], gd[2] = low, d2
    gb[2] = fwd_xy(m, d2)


def gather_ahead(m, recv, ga, gb, gc, gd):
    at_zp, at_tp = recv[1], recv[3]
    a0, d0, low = ga[0], gd[0], ga[1]
    gb[0] = pick(m["low"], fwd_x(d0), pick(m["near"], rows(d0, -2), rows(at_zp, 2)))
    gc[0] = pick(m["low"], fwd_y(m, a0), pick(m["even"], rows(a0, -1), rows(at_tp, 1)))
    up_z = pick(m["near"], rows(low, -2), at_zp)
    up_t = pick(m["even"], rows(low, -1), at_tp)
    gc[1] = pick(m["low"], up_z, up_t)
    gc[2] = pick(m["low"], up_t, up_z)


def gather_behind(m, recv, corner, ga, gb, gd):
    at_zm, at_tm = recv[0], recv[2]
    diag = corner[...]
    row = m["row"]
    dz = pick(row < 2, rows(at_zm, -2), pick(row < 4, at_zm, pick(row < 6, rows(at_zm, 2), rows(at_zm, 4))))
    ga[3], gd[3] = at_zm, dz
    gb[3] = pick(row < 6, fwd_xy(m, dz), pick(m["even"], rows(at_zm, 3), rows(diag, 6)))
    dt = pick(m["low"], pick(m["even"], rows(at_tm, 3), rows(at_tm, 4)), pick(m["even"], rows(at_tm, -1), at_tm))
    ga[4], gd[4] = at_tm, dt
    gb[4] = pick(m["even"], fwd_xy(m, dt), pick(row < 2, rows(at_tm, 2), diag))


def scatter_own(m, pa, pb, pc, pd):
    a0, b0, c0, d0 = pa[0], pb[0], pc[0], pd[0]
    c1, c2 = pc[1], pc[2]
    zero = jnp.zeros_like(a0)
    from_z = pick(m["near"], zero, rows(pick(m["low"], c1, c2), 2))
    from_t = pick(m["even"], zero, rows(pick(m["low"], c2, c1), 1))
    low = (pa[1] + pa[2]) + (from_z + from_t)
    low = low + pick(m["low"], a0 + back_y(m, c0), rows(d0 + back_x(b0), 4))
    high = (pd[1] + back_xy(m, pb[1])) + rows(pd[2] + back_xy(m, pb[2]), 4)
    z_part = a0 + pick(m["even"], zero, rows(c0, 1))
    t_part = d0 + pick(m["near"], zero, rows(b0, 2))
    return low, high + pick(m["low"], rows(z_part, 4), t_part)


def scatter_rim(m, rim):
    rz, rt = rim[0], rim[1]
    zero = jnp.zeros_like(rz)
    low = pick(m["near"], rz, zero) + pick(m["even"], rt, zero)
    high = pick(m["low"], pick(m["even"], rows(rt, -1), zero), pick(m["near"], rows(rz, -2), zero))
    return low, high


def each(first, last, body):
    def step(k, carry):
        body(k)
        return carry

    lax.fori_loop(first, last, step, 0)


def staples_own(ga, gb, gd, keep_t, pc):
    def corner_products(k):
        keep_t[k] = join(mul_dn(split(ga[k]), split(gd[k])))

    def ends(k):
        pc[k] = join(mul_dn(split(keep_t[k]), split(gb[k])))

    each(0, 3, corner_products)
    each(1, 3, ends)


def staples_ahead(ga, gb, gc, gd, keep_t, keep_z, pa, pb, pc, pd):
    pc[0] = join(mul_dn(split(keep_t[0]), split(gb[0])))

    def block(k):
        c = split(gc[k])
        pb[k] = join(mul(split(keep_t[k]), c))
        z = mul_nd(c, split(gb[k]))
        keep_z[k] = join(z)
        pa[k] = join(mul(split(gd[k]), z))
        pd[k] = join(mul_nd(split(ga[k]), z))

    each(0, 3, block)


def staples_behind(ga, gb, gd, keep_t, rim):
    def block(k):
        t = mul_dn(split(ga[k]), split(gd[k]))
        keep_t[k] = join(t)
        rim[k - 3] = join(mul_dn(t, split(gb[k])))

    each(3, 5, block)


def forces_own(ga, gb, gd, keep_t, keep_z, sa, sd, wa, wb, wd, keep_n, zb, pa, pc, pd):
    def block(k):
        va, vd = wa[k], wd[k]
        keep_n[k] = join(mul_dn(split(ga[k]), mul(skew_matrix(va - vd), split(gd[k]))))
        pa[k] = join(mul(skew_matrix(vd), split(sa[k])))
        pd[k] = join(mul(skew_matrix(va), split(sd[k])))

    each(0, 3, block)
    each(1, 3, lambda k: force_end(gb, keep_t, keep_z, wb, keep_n, zb, pc, k))


def force_end(gb, keep_t, keep_z, wb, keep_n, zb, pc, k):
    ob = skew_matrix(wb[k])
    pc[k] = join(mul(sub(mul_dn(split(keep_t[k]), ob), dagger(split(keep_n[k]))), split(gb[k])))
    zb[k] = join(mul(split(keep_z[k]), ob))


def forces_ahead(ga, gb, gc, gd, keep_t, keep_z, wb, wc, keep_n, zb, pa, pb, pc, pd):
    force_end(gb, keep_t, keep_z, wb, keep_n, zb, pc, 0)

    def block(k):
        oc = skew_matrix(wc[k])
        pb[k] = join(mul(sub(mul(split(keep_t[k]), oc), split(keep_n[k])), split(gc[k])))
        q = sub(mul(oc, split(keep_z[k])), split(zb[k]))
        pa[k] = join(add(mul(split(gd[k]), q), split(pa[k])))
        pd[k] = join(add(mul_nd(split(ga[k]), q), split(pd[k])))

    each(0, 3, block)


def forces_behind(ga, gb, gd, keep_t, wa, wb, wd, rim):
    def block(k):
        n = mul_dn(split(ga[k]), mul(skew_matrix(wa[k] - wd[k]), split(gd[k])))
        t = split(keep_t[k])
        rim[k - 3] = join(mul(sub(mul_dn(t, skew_matrix(wb[k])), dagger(n)), split(gb[k])))

    each(3, 5, block)


def weights(h):
    hh = h * h
    r2 = 1.0 - hh * 0.5
    r4 = r2 + hh * hh * (1.0 / 24.0)
    r6 = r4 - hh * hh * hh * (1.0 / 720.0)
    i3 = h - h * hh * (1.0 / 6.0)
    i5 = i3 + h * hh * hh * (1.0 / 120.0)
    return (r6, i5), (r4, i5), (r4, i3), (r2, i3), (r2, h)


def exponent_parts(links, staple_sum, keep_b, keep_bb, keep_e, keep_s):
    def block(k, carry):
        u, c = split(links[k]), split(staple_sum[k])
        omega = mul_nd(c, u)
        parts = [WEIGHT * v for v in skew_parts(omega)]
        h = (parts[0] + parts[1] + parts[2]) * (1.0 / 3.0)
        parts = jnp.stack([v - h for v in parts[:3]] + parts[3:])
        b = skew_matrix(parts)
        bb = mul(b, b)
        p = 0.5 * (bb[0][0, 0] + bb[0][1, 1] + bb[0][2, 2])
        s = jnp.sum((b[1] * bb[0] - b[0] * bb[1]).reshape(9, 8, LANES), axis=0) * (1.0 / 3.0)
        w0, w1, w2, w3, w4 = weights(h)
        pp, ps = p * p, p * s
        f0 = (
            w0[0] - s * w3[1] * (1.0 / 6.0) - ps * h * (1.0 / 120.0) - s * s * (1.0 / 720.0),
            w0[1] + s * w3[0] * (1.0 / 6.0) + ps * (1.0 / 120.0),
        )
        f1 = (
            w1[0] + p * w3[0] * (1.0 / 6.0) - s * w4[1] * (1.0 / 24.0) + pp * (1.0 / 120.0),
            w1[1] + p * w3[1] * (1.0 / 6.0) + s * w4[0] * (1.0 / 24.0) + pp * h * (1.0 / 120.0) + ps * (1.0 / 360.0),
        )
        f2 = (
            w2[0] * 0.5 + p * w4[0] * (1.0 / 24.0) - s * h * (1.0 / 120.0) + pp * (1.0 / 720.0),
            w2[1] * 0.5 + p * w4[1] * (1.0 / 24.0) + s * (1.0 / 120.0),
        )
        e = add(scaled(f1, b), scaled(f2, bb))
        unit = [[jnp.ones_like(p) if i == j else jnp.zeros_like(p) for j in range(3)] for i in range(3)]
        unit = jnp.stack([jnp.stack(r) for r in unit])
        e = e[0] + f0[0] * unit, e[1] + f0[1] * unit
        keep_b[k] = parts
        keep_bb[k] = join(bb)
        keep_e[k] = join(e)
        keep_s[k] = jnp.stack([p, s, h, f1[0], f1[1], f2[0], f2[1]])
        return carry

    lax.fori_loop(0, 2, block, 0)


def force_products(links, force, keep_d):
    def block(k):
        keep_d[k] = join(mul_nd(split(force[k]), split(links[k])))

    each(0, 2, block)


def exponent_forces(keep_d, keep_b, keep_bb, keep_s, omega):
    def block(k, carry):
        b, bb = skew_matrix(keep_b[k]), split(keep_bb[k])
        kept = keep_s[k]
        p, s, h = kept[0], kept[1], kept[2]
        f1, f2 = (kept[3], -kept[4]), (kept[5], -kept[6])
        d = split(keep_d[k])

        def overlap(x):
            re = jnp.sum((d[0] * x[0] + d[1] * x[1]).reshape(9, 8, LANES), axis=0)
            im = jnp.sum((d[0] * x[1] - d[1] * x[0]).reshape(9, 8, LANES), axis=0)
            return re, im

        t0 = d[0][0, 0] + d[0][1, 1] + d[0][2, 2], -(d[1][0, 0] + d[1][1, 1] + d[1][2, 2])
        t1, t2 = overlap(b), overlap(bb)
        w0, w1, w2, w3, w4 = weights(h)
        pp, ps = p * p, p * s

        def slope(*changes):
            total = None
            for t, (re, im) in zip((t0, t1, t2), changes):
                term = t[0] * re - t[1] * im
                total = term if total is None else total + term
            return total

        gp = slope(
            (-s * h * (1.0 / 120.0), s * (1.0 / 120.0)),
            (w3[0] * (1.0 / 6.0) + p * (1.0 / 60.0), w3[1] * (1.0 / 6.0) + p * h * (1.0 / 60.0) + s * (1.0 / 360.0)),
            (w4[0] * (1.0 / 24.0) + p * (1.0 / 360.0), w4[1] * (1.0 / 24.0)),
        )
        gs = slope(
            (
                -w3[1] * (1.0 / 6.0) - p * h * (1.0 / 120.0) - s * (1.0 / 360.0),
                w3[0] * (1.0 / 6.0) + p * (1.0 / 120.0),
            ),
            (-w4[1] * (1.0 / 24.0), w4[0] * (1.0 / 24.0) + p * (1.0 / 360.0)),
            (-h * (1.0 / 120.0), jnp.full_like(h, 1.0 / 120.0)),
        )
        x0 = w1[0] - s * w4[1] * (1.0 / 6.0), w1[1] + s * w4[0] * (1.0 / 6.0) + ps * (1.0 / 120.0)
        x1 = (
            w2[0] + p * w4[0] * (1.0 / 6.0) - s * h * (1.0 / 24.0) + pp * (1.0 / 120.0),
            w2[1] + p * w4[1] * (1.0 / 6.0) + s * (1.0 / 24.0),
        )
        x2 = w3[0] * 0.5 + p * (1.0 / 24.0), w3[1] * 0.5 + p * h * (1.0 / 24.0) + s * (1.0 / 120.0)
        gh = slope(*[(-x[1], x[0]) for x in (x0, x1, x2)])
        d2 = scaled(f2, d)
        back = dagger(d2)
        half = 0.5 * (d2[0] + back[0]), 0.5 * (d2[1] + back[1])
        n = mul(b, half)
        d1 = scaled(f1, d)
        whole = (
            d1[0] - 2.0 * n[0] - gp * b[0] - gs * bb[1],
            d1[1] - 2.0 * n[1] - gp * b[1] + gs * bb[0],
        )
        parts = skew_parts(whole)
        shift = (gh - (parts[0] + parts[1] + parts[2])) * (1.0 / 3.0)
        parts = jnp.stack([WEIGHT * (v + shift) for v in parts[:3]] + [WEIGHT * v for v in parts[3:]])
        omega[k] = parts
        return carry

    lax.fori_loop(0, 2, block, 0)


def direct_forces(staple_sum, force, keep_e, omega, direct):
    def block(k):
        own = mul_dn(split(keep_e[k]), split(force[k]))
        direct[k] = join(sub(own, mul(skew_matrix(omega[k]), split(staple_sum[k]))))

    each(0, 2, block)


def kernel(counts, base_hbm, smeared_hbm, force_hbm, out_ref, links, force, csum, direct, ga, gb, gc, gd, wa, wb, wc, wd,
           keep_t, keep_z, sa, sd, keep_n, zb, pa, pb, pc, pd, rim, keep_b, keep_bb, keep_e, keep_s, keep_d, omega,
           recv_u, corner_u, send_w, recv_w, corner_w, in_sem, send_u_sem, recv_u_sem, send_w_sem, recv_w_sem):
    n_gz, n_ta = counts
    gz, ta = lax.axis_index("gz"), lax.axis_index("ta")
    zp, zm = lax.rem(gz + 1, n_gz), lax.rem(gz + n_gz - 1, n_gz)
    tp, tm = lax.rem(ta + 1, n_ta), lax.rem(ta + n_ta - 1, n_ta)
    where = ((zp, ta), (zm, ta), (gz, tp), (gz, tm), (zp, tm), (zm, tp))

    barrier = pltpu.get_barrier_semaphore()
    for device in where:
        pl.semaphore_signal(barrier, inc=1, device_id=device, device_id_type=MESH)

    def fetch(src, dst, slot):
        return [
            pltpu.make_async_copy(src.at[k], dst.at[k // 2, :, pl.ds(k % 2 * 4, 4)], in_sem.at[slot, k])
            for k in range(4)
        ]

    fetches = fetch(smeared_hbm, links.at[0], 0) + fetch(base_hbm, links.at[1], 1) + fetch(force_hbm, force, 2)
    for copy in fetches:
        copy.start()
    m = masks()
    moves_u = [
        link_copies(
            src, recv_u.at[level], corner_u.at[level], (send_u_sem.at[level], recv_u_sem.at[level]), where
        )
        for level, src in ((0, smeared_hbm), (1, base_hbm))
    ]
    pl.semaphore_wait(barrier, 6)
    start(moves_u[0])
    for copy in fetches:
        copy.wait()

    def of(level, *refs):
        return [r.at[level] for r in refs]

    def sent(moves):
        for copy in moves[0] + moves[1]:
            copy.wait_send()

    def landed(copies):
        for copy in copies:
            copy.wait_recv()

    def before(level):
        la, lb, ld, lt = of(level, ga, gb, gd, keep_t)
        gather_own(m, links[level, 0], links[level, 1], la, lb, ld)
        staples_own(la, lb, ld, lt, pc.at[level])

    def forward(level):
        la, lb, lc, ld, lt, lz = of(level, ga, gb, gc, gd, keep_t, keep_z)
        ahead, behind = moves_u[level]
        landed(ahead)
        gather_ahead(m, recv_u.at[level], la, lb, lc, ld)
        staples_ahead(la, lb, lc, ld, lt, lz, sa.at[level], pb, pc.at[level], sd.at[level])
        csum[level, 0], csum[level, 1] = scatter_own(m, sa.at[level], pb, pc.at[level], sd.at[level])
        landed(behind)
        gather_behind(m, recv_u.at[level], corner_u.at[level], la, lb, ld)
        staples_behind(la, lb, ld, lt, rim)
        low, high = scatter_rim(m, rim)
        csum[level, 0] += low
        csum[level, 1] += high
        exponent_parts(links.at[level], csum.at[level], *of(level, keep_b, keep_bb, keep_e, keep_s))

    def send_force(level):
        exponent_forces(keep_d, *of(level, keep_b, keep_bb, keep_s, omega))
        pack_sends(m, omega[level, 0], omega[level, 1], SKEW, send_w.at[level])
        moves = term_copies(
            omega.at[level], send_w.at[level], recv_w.at[level], corner_w.at[level],
            (send_w_sem.at[level], recv_w_sem.at[level]), where,
        )
        start(moves)
        return moves

    def finish(level, moves, meanwhile):
        la, lb, lc, ld, lt, lz = of(level, ga, gb, gc, gd, keep_t, keep_z)
        direct_forces(csum.at[level], force, keep_e.at[level], omega.at[level], direct)
        gather_own(m, omega[level, 0], omega[level, 1], wa, wb, wd)
        forces_own(la, lb, ld, lt, lz, sa.at[level], sd.at[level], wa, wb, wd, keep_n, zb, pa, pc.at[level], pd)
        meanwhile()
        ahead, behind = moves
        landed(ahead)
        gather_ahead(m, recv_w.at[level], wa, wb, wc, wd)
        forces_ahead(la, lb, lc, ld, lt, lz, wb, wc, keep_n, zb, pa, pb, pc.at[level], pd)
        low, high = scatter_own(m, pa, pb, pc.at[level], pd)
        direct[0] += low
        direct[1] += high
        landed(behind)
        gather_behind(m, recv_w.at[level], corner_w.at[level], wa, wb, wd)
        forces_behind(la, lb, ld, lt, wa, wb, wd, rim)
        low, high = scatter_rim(m, rim)
        low, high = low + direct[0], high + direct[1]
        if level == 0:
            force[0], force[1] = low, high
        else:
            out_ref[0], out_ref[1] = low[:, :4], low[:, 4:]
            out_ref[2], out_ref[3] = high[:, :4], high[:, 4:]

    force_products(links.at[0], force, keep_d)
    before(0)
    before(1)
    sent(moves_u[0])
    start(moves_u[1])
    forward(0)
    moves_w0 = send_force(0)
    finish(0, moves_w0, lambda: forward(1))
    force_products(links.at[1], force, keep_d)
    moves_w1 = send_force(1)
    finish(1, moves_w1, lambda: None)
    for moves in (moves_u[1], moves_w0, moves_w1):
        sent(moves)


def solution(mesh):
    counts = (mesh.shape["gz"], mesh.shape["ta"])

    def vmem(*shape):
        return pltpu.VMEM(shape + (8, LANES), jnp.float32)

    def per_device(base_links, smeared_links, top_force):
        def flat(v):
            return v.reshape(4, LINK, 4, LANES)

        out = pl.pallas_call(
            lambda *refs: kernel(counts, *refs),
            out_shape=jax.ShapeDtypeStruct((4, LINK, 4, LANES), jnp.float32),
            in_specs=[pl.BlockSpec(memory_space=pl.ANY)] * 3,
            out_specs=pl.BlockSpec(memory_space=pltpu.VMEM),
            scratch_shapes=[
                vmem(2, 2, LINK),
                vmem(2, LINK),
                vmem(2, 2, LINK),
                vmem(2, LINK),
                vmem(2, 5, LINK),
                vmem(2, 5, LINK),
                vmem(2, 3, LINK),
                vmem(2, 5, LINK),
                vmem(5, SKEW),
                vmem(5, SKEW),
                vmem(3, SKEW),
                vmem(5, SKEW),
                vmem(2, 5, LINK),
                vmem(2, 3, LINK),
                vmem(2, 3, LINK),
                vmem(2, 3, LINK),
                vmem(3, LINK),
                vmem(3, LINK),
                vmem(3, LINK),
                vmem(3, LINK),
                vmem(2, 3, LINK),
                vmem(3, LINK),
                vmem(2, LINK),
                vmem(2, 2, SKEW),
                vmem(2, 2, LINK),
                vmem(2, 2, LINK),
                vmem(2, 2, 7),
                vmem(2, LINK),
                vmem(2, 2, SKEW),
                vmem(2, 4, LINK),
                vmem(2, LINK),
                vmem(2, 4, SKEW),
                vmem(2, 4, SKEW),
                vmem(2, SKEW),
                pltpu.SemaphoreType.DMA((3, 4)),
                pltpu.SemaphoreType.DMA((2, 23)),
                pltpu.SemaphoreType.DMA((2, 23)),
                pltpu.SemaphoreType.DMA((2, 6)),
                pltpu.SemaphoreType.DMA((2, 6)),
            ],
            compiler_params=pltpu.CompilerParams(
                collective_id=0, has_side_effects=True, vmem_limit_bytes=48 * 1024 * 1024
            ),
            name="stout_back",
        )(*[pltpu.with_memory_space_constraint(flat(v), pltpu.HBM) for v in (base_links, smeared_links, top_force)])
        return out.reshape(base_links.shape)

    spec = P(None, None, None, None, "gz", "ta", None)
    return jax.shard_map(per_device, mesh=mesh, in_specs=(spec, spec, spec), out_specs=spec, check_vma=False)
```

```python
import jax
import jax.numpy as jnp
from jax import lax
from jax.experimental import pallas as pl
from jax.experimental.pallas import tpu as pltpu
from jax.sharding import PartitionSpec as P

MESH = pl.DeviceIdType.MESH
LY = 8
WEIGHT = 0.1
LANES = 128
LINK = 18
SKEW = 9


def masks():
    row = lax.broadcasted_iota(jnp.int32, (1, 8, LANES), 1)
    col = lax.broadcasted_iota(jnp.int32, (1, 8, LANES), 2) % LY
    return {
        "low": row < 4,
        "even": row % 2 == 0,
        "near": row % 4 < 2,
        "row": row,
        "first": col == 0,
        "last": col == LY - 1,
    }


def pick(mask, yes, no):
    return jnp.where(jnp.broadcast_to(mask, yes.shape), yes, no)


def rows(v, shift):
    return pltpu.roll(v, shift % 8, 1)


def fwd_x(v):
    return pltpu.roll(v, LANES - LY, 2)


def back_x(v):
    return pltpu.roll(v, LY, 2)


def fwd_y(m, v):
    return pick(m["last"], pltpu.roll(v, LY - 1, 2), pltpu.roll(v, LANES - 1, 2))


def back_y(m, v):
    return pick(m["first"], pltpu.roll(v, LANES - LY + 1, 2), pltpu.roll(v, 1, 2))


def fwd_xy(m, v):
    return pick(m["low"], fwd_x(v), fwd_y(m, v))


def back_xy(m, v):
    return pick(m["low"], back_x(v), back_y(m, v))


def split(v):
    return v[:9].reshape(3, 3, 8, LANES), v[9:].reshape(3, 3, 8, LANES)


def join(m):
    return jnp.concatenate([m[0].reshape(9, 8, LANES), m[1].reshape(9, 8, LANES)], axis=0)


def outer_sum(lefts, rights):
    total = None
    for left, right in zip(lefts, rights):
        term = left[:, None] * right[None, :]
        total = term if total is None else total + term
    return total


def columns(a):
    return [a[:, k] for k in range(3)]


def lines(a):
    return [a[k] for k in range(3)]


def product(left, right, sl, sr):
    (ar, ai), (br, bi) = left, right
    rr, ii = outer_sum(ar, br), outer_sum(ai, bi)
    ri, ir = outer_sum(ar, bi), outer_sum(ai, br)
    re = rr - ii if sl * sr > 0 else rr + ii
    if sl > 0 and sr > 0:
        im = ri + ir
    elif sl < 0 and sr > 0:
        im = ri - ir
    else:
        im = ir - ri
    return re, im


def mul(a, b):
    return product((columns(a[0]), columns(a[1])), (lines(b[0]), lines(b[1])), 1, 1)


def mul_dn(a, b):
    return product((lines(a[0]), lines(a[1])), (lines(b[0]), lines(b[1])), -1, 1)


def mul_nd(a, b):
    return product((columns(a[0]), columns(a[1])), (columns(b[0]), columns(b[1])), 1, -1)


def add(a, b):
    return a[0] + b[0], a[1] + b[1]


def sub(a, b):
    return a[0] - b[0], a[1] - b[1]


def flip(v):
    return jnp.stack([v[:, 0], v[:, 1], v[:, 2]], axis=0)


def dagger(a):
    return flip(a[0]), -flip(a[1])


def scaled(c, a):
    cr, ci = c
    return cr * a[0] - ci * a[1], cr * a[1] + ci * a[0]


def skew_parts(a):
    re, im = a
    out = [im[0, 0], im[1, 1], im[2, 2]]
    for i, j in ((0, 1), (0, 2), (1, 2)):
        out += [0.5 * (re[i, j] - re[j, i]), 0.5 * (im[i, j] + im[j, i])]
    return out


def skew_matrix(v):
    d0, d1, d2, r01, i01, r02, i02, r12, i12 = [v[k] for k in range(9)]
    zero = jnp.zeros_like(d0)
    re = jnp.stack([jnp.stack([zero, r01, r02]), jnp.stack([-r01, zero, r12]), jnp.stack([-r02, -r12, zero])])
    im = jnp.stack([jnp.stack([d0, i01, i02]), jnp.stack([i01, d1, i12]), jnp.stack([i02, i12, d2])])
    return re, im


def pack_sends(m, low, high, comps, send):
    send[0, :comps] = pick(m["near"], rows(low, -2), high)
    send[1, :comps] = pick(m["near"], high, rows(low, 2))
    send[2, :comps] = pick(m["even"], rows(low, -1), high)
    send[3, :comps] = pick(m["even"], rows(high, 4), rows(low, 1))


def remote(src, dst, sems, k, device):
    return pltpu.make_async_remote_copy(
        src_ref=src, dst_ref=dst, send_sem=sems[0].at[k], recv_sem=sems[1].at[k], device_id=device, device_id_type=MESH
    )


def link_copies(src, recv, corner, sems, where):
    ahead, behind = [], []
    k = 0

    def put(out, direction, row, count, slot, to):
        nonlocal k
        dst = corner if slot > 3 else recv.at[slot]
        out.append(
            remote(src.at[direction, :, pl.ds(row, count)], dst.at[:, pl.ds(to, count)], sems, k, where[slot])
        )
        k += 1

    put(behind, 2, 2, 1, 4, 1)
    put(behind, 3, 1, 1, 5, 3)
    for direction, to in ((0, 1), (1, 5), (2, 4)):
        put(ahead, direction, 0, 1, 3, to)
        put(ahead, direction, 2, 1, 3, to + 2)
    for direction, to in ((0, 2), (1, 6), (3, 4)):
        put(ahead, direction, 0, 2, 1, to)
    for direction, to in ((0, 0), (2, 1), (1, 4), (3, 5)):
        put(behind, direction, 1, 1, 2, to)
        put(behind, direction, 3, 1, 2, to + 2)
    for direction, to in ((0, 0), (2, 2), (1, 4), (3, 6)):
        put(behind, direction, 2, 2, 0, to)
    return ahead, behind


def term_copies(src, send, recv, corner, sems, where):
    behind = [
        remote(src.at[1, :, pl.ds(2, 1)], corner.at[:, pl.ds(1, 1)], sems, 4, where[4]),
        remote(src.at[1, :, pl.ds(5, 1)], corner.at[:, pl.ds(3, 1)], sems, 5, where[5]),
        remote(send.at[0], recv.at[0], sems, 0, where[0]),
        remote(send.at[2], recv.at[2], sems, 2, where[2]),
    ]
    ahead = [
        remote(send.at[1, :, pl.ds(2, 6)], recv.at[1, :, pl.ds(2, 6)], sems, 1, where[1]),
        remote(send.at[3, :, pl.ds(1, 1)], recv.at[3, :, pl.ds(1, 1)], sems, 3, where[3]),
        remote(send.at[3, :, pl.ds(3, 5)], recv.at[3, :, pl.ds(3, 5)], sems, 6, where[3]),
    ]
    return ahead, behind


def start(moves):
    ahead, behind = moves
    for copy in behind[:2] + ahead + behind[2:]:
        copy.start()


def gather_own(m, low, high, ga, gb, gd):
    ga[0], gd[0] = pick(m["low"], low, rows(high, 4)), pick(m["low"], rows(low, 4), high)
    ga[1], gd[1] = low, high
    gb[1] = fwd_xy(m, high)
    d2 = rows(high, 4)
    ga[2], gd[2] = low, d2
    gb[2] = fwd_xy(m, d2)


def gather_ahead(m, recv, ga, gb, gc, gd):
    at_zp, at_tp = recv[1], recv[3]
    a0, d0, low = ga[0], gd[0], ga[1]
    gb[0] = pick(m["low"], fwd_x(d0), pick(m["near"], rows(d0, -2), rows(at_zp, 2)))
    gc[0] = pick(m["low"], fwd_y(m, a0), pick(m["even"], rows(a0, -1), rows(at_tp, 1)))
    up_z = pick(m["near"], rows(low, -2), at_zp)
    up_t = pick(m["even"], rows(low, -1), at_tp)
    gc[1] = pick(m["low"], up_z, up_t)
    gc[2] = pick(m["low"], up_t, up_z)


def gather_behind(m, recv, corner, ga, gb, gd):
    at_zm, at_tm = recv[0], recv[2]
    diag = corner[...]
    row = m["row"]
    dz = pick(row < 2, rows(at_zm, -2), pick(row < 4, at_zm, pick(row < 6, rows(at_zm, 2), rows(at_zm, 4))))
    ga[3], gd[3] = at_zm, dz
    gb[3] = pick(row < 6, fwd_xy(m, dz), pick(m["even"], rows(at_zm, 3), rows(diag, 6)))
    dt = pick(m["low"], pick(m["even"], rows(at_tm, 3), rows(at_tm, 4)), pick(m["even"], rows(at_tm, -1), at_tm))
    ga[4], gd[4] = at_tm, dt
    gb[4] = pick(m["even"], fwd_xy(m, dt), pick(row < 2, rows(at_tm, 2), diag))


def scatter_own(m, pa, pb, pc, pd):
    a0, b0, c0, d0 = pa[0], pb[0], pc[0], pd[0]
    c1, c2 = pc[1], pc[2]
    zero = jnp.zeros_like(a0)
    from_z = pick(m["near"], zero, rows(pick(m["low"], c1, c2), 2))
    from_t = pick(m["even"], zero, rows(pick(m["low"], c2, c1), 1))
    low = (pa[1] + pa[2]) + (from_z + from_t)
    low = low + pick(m["low"], a0 + back_y(m, c0), rows(d0 + back_x(b0), 4))
    high = (pd[1] + back_xy(m, pb[1])) + rows(pd[2] + back_xy(m, pb[2]), 4)
    z_part = a0 + pick(m["even"], zero, rows(c0, 1))
    t_part = d0 + pick(m["near"], zero, rows(b0, 2))
    return low, high + pick(m["low"], rows(z_part, 4), t_part)


def scatter_rim(m, rim):
    rz, rt = rim[0], rim[1]
    zero = jnp.zeros_like(rz)
    low = pick(m["near"], rz, zero) + pick(m["even"], rt, zero)
    high = pick(m["low"], pick(m["even"], rows(rt, -1), zero), pick(m["near"], rows(rz, -2), zero))
    return low, high


def each(first, last, body):
    def step(k, carry):
        body(k)
        return carry

    lax.fori_loop(first, last, step, 0)


def staples_own(ga, gb, gd, keep_t, pc):
    def corner_products(k):
        keep_t[k] = join(mul_dn(split(ga[k]), split(gd[k])))

    def ends(k):
        pc[k] = join(mul_dn(split(keep_t[k]), split(gb[k])))

    each(0, 3, corner_products)
    each(1, 3, ends)


def staples_ahead(ga, gb, gc, gd, keep_t, keep_z, pa, pb, pc, pd):
    pc[0] = join(mul_dn(split(keep_t[0]), split(gb[0])))

    def block(k):
        c = split(gc[k])
        pb[k] = join(mul(split(keep_t[k]), c))
        z = mul_nd(c, split(gb[k]))
        keep_z[k] = join(z)
        pa[k] = join(mul(split(gd[k]), z))
        pd[k] = join(mul_nd(split(ga[k]), z))

    each(0, 3, block)


def staples_behind(ga, gb, gd, keep_t, rim):
    def block(k):
        t = mul_dn(split(ga[k]), split(gd[k]))
        keep_t[k] = join(t)
        rim[k - 3] = join(mul_dn(t, split(gb[k])))

    each(3, 5, block)


def forces_own(ga, gb, gd, keep_t, keep_z, sa, sd, wa, wb, wd, keep_n, zb, pa, pc, pd):
    def block(k):
        va, vd = wa[k], wd[k]
        keep_n[k] = join(mul_dn(split(ga[k]), mul(skew_matrix(va - vd), split(gd[k]))))
        pa[k] = join(mul(skew_matrix(vd), split(sa[k])))
        pd[k] = join(mul(skew_matrix(va), split(sd[k])))

    each(0, 3, block)
    each(1, 3, lambda k: force_end(gb, keep_t, keep_z, wb, keep_n, zb, pc, k))


def force_end(gb, keep_t, keep_z, wb, keep_n, zb, pc, k):
    ob = skew_matrix(wb[k])
    pc[k] = join(mul(sub(mul_dn(split(keep_t[k]), ob), dagger(split(keep_n[k]))), split(gb[k])))
    zb[k] = join(mul(split(keep_z[k]), ob))


def forces_ahead(ga, gb, gc, gd, keep_t, keep_z, wb, wc, keep_n, zb, pa, pb, pc, pd):
    force_end(gb, keep_t, keep_z, wb, keep_n, zb, pc, 0)

    def block(k):
        oc = skew_matrix(wc[k])
        pb[k] = join(mul(sub(mul(split(keep_t[k]), oc), split(keep_n[k])), split(gc[k])))
        q = sub(mul(oc, split(keep_z[k])), split(zb[k]))
        pa[k] = join(add(mul(split(gd[k]), q), split(pa[k])))
        pd[k] = join(add(mul_nd(split(ga[k]), q), split(pd[k])))

    each(0, 3, block)


def forces_behind(ga, gb, gd, keep_t, wa, wb, wd, rim):
    def block(k):
        n = mul_dn(split(ga[k]), mul(skew_matrix(wa[k] - wd[k]), split(gd[k])))
        t = split(keep_t[k])
        rim[k - 3] = join(mul(sub(mul_dn(t, skew_matrix(wb[k])), dagger(n)), split(gb[k])))

    each(3, 5, block)


def weights(h):
    hh = h * h
    r2 = 1.0 - hh * 0.5
    r4 = r2 + hh * hh * (1.0 / 24.0)
    r6 = r4 - hh * hh * hh * (1.0 / 720.0)
    i3 = h - h * hh * (1.0 / 6.0)
    i5 = i3 + h * hh * hh * (1.0 / 120.0)
    return (r6, i5), (r4, i5), (r4, i3), (r2, i3), (r2, h)


def exponent_parts(links, staple_sum, keep_b, keep_bb, keep_e, keep_s):
    def block(k, carry):
        u, c = split(links[k]), split(staple_sum[k])
        omega = mul_nd(c, u)
        parts = [WEIGHT * v for v in skew_parts(omega)]
        h = (parts[0] + parts[1] + parts[2]) * (1.0 / 3.0)
        parts = jnp.stack([v - h for v in parts[:3]] + parts[3:])
        b = skew_matrix(parts)
        bb = mul(b, b)
        p = 0.5 * (bb[0][0, 0] + bb[0][1, 1] + bb[0][2, 2])
        s = jnp.sum((b[1] * bb[0] - b[0] * bb[1]).reshape(9, 8, LANES), axis=0) * (1.0 / 3.0)
        w0, w1, w2, w3, w4 = weights(h)
        pp, ps = p * p, p * s
        f0 = (
            w0[0] - s * w3[1] * (1.0 / 6.0) - ps * h * (1.0 / 120.0) - s * s * (1.0 / 720.0),
            w0[1] + s * w3[0] * (1.0 / 6.0) + ps * (1.0 / 120.0),
        )
        f1 = (
            w1[0] + p * w3[0] * (1.0 / 6.0) - s * w4[1] * (1.0 / 24.0) + pp * (1.0 / 120.0),
            w1[1] + p * w3[1] * (1.0 / 6.0) + s * w4[0] * (1.0 / 24.0) + pp * h * (1.0 / 120.0) + ps * (1.0 / 360.0),
        )
        f2 = (
            w2[0] * 0.5 + p * w4[0] * (1.0 / 24.0) - s * h * (1.0 / 120.0) + pp * (1.0 / 720.0),
            w2[1] * 0.5 + p * w4[1] * (1.0 / 24.0) + s * (1.0 / 120.0),
        )
        e = add(scaled(f1, b), scaled(f2, bb))
        unit = [[jnp.ones_like(p) if i == j else jnp.zeros_like(p) for j in range(3)] for i in range(3)]
        unit = jnp.stack([jnp.stack(r) for r in unit])
        e = e[0] + f0[0] * unit, e[1] + f0[1] * unit
        keep_b[k] = parts
        keep_bb[k] = join(bb)
        keep_e[k] = join(e)
        keep_s[k] = jnp.stack([p, s, h, f1[0], f1[1], f2[0], f2[1]])
        return carry

    lax.fori_loop(0, 2, block, 0)


def force_products(links, force, keep_d):
    def block(k):
        keep_d[k] = join(mul_nd(split(force[k]), split(links[k])))

    each(0, 2, block)


def exponent_forces(keep_d, keep_b, keep_bb, keep_s, omega):
    def block(k, carry):
        b, bb = skew_matrix(keep_b[k]), split(keep_bb[k])
        kept = keep_s[k]
        p, s, h = kept[0], kept[1], kept[2]
        f1, f2 = (kept[3], -kept[4]), (kept[5], -kept[6])
        d = split(keep_d[k])

        def overlap(x):
            re = jnp.sum((d[0] * x[0] + d[1] * x[1]).reshape(9, 8, LANES), axis=0)
            im = jnp.sum((d[0] * x[1] - d[1] * x[0]).reshape(9, 8, LANES), axis=0)
            return re, im

        t0 = d[0][0, 0] + d[0][1, 1] + d[0][2, 2], -(d[1][0, 0] + d[1][1, 1] + d[1][2, 2])
        t1, t2 = overlap(b), overlap(bb)
        w0, w1, w2, w3, w4 = weights(h)
        pp, ps = p * p, p * s

        def slope(*changes):
            total = None
            for t, (re, im) in zip((t0, t1, t2), changes):
                term = t[0] * re - t[1] * im
                total = term if total is None else total + term
            return total

        gp = slope(
            (-s * h * (1.0 / 120.0), s * (1.0 / 120.0)),
            (w3[0] * (1.0 / 6.0) + p * (1.0 / 60.0), w3[1] * (1.0 / 6.0) + p * h * (1.0 / 60.0) + s * (1.0 / 360.0)),
            (w4[0] * (1.0 / 24.0) + p * (1.0 / 360.0), w4[1] * (1.0 / 24.0)),
        )
        gs = slope(
            (
                -w3[1] * (1.0 / 6.0) - p * h * (1.0 / 120.0) - s * (1.0 / 360.0),
                w3[0] * (1.0 / 6.0) + p * (1.0 / 120.0),
            ),
            (-w4[1] * (1.0 / 24.0), w4[0] * (1.0 / 24.0) + p * (1.0 / 360.0)),
            (-h * (1.0 / 120.0), jnp.full_like(h, 1.0 / 120.0)),
        )
        x0 = w1[0] - s * w4[1] * (1.0 / 6.0), w1[1] + s * w4[0] * (1.0 / 6.0) + ps * (1.0 / 120.0)
        x1 = (
            w2[0] + p * w4[0] * (1.0 / 6.0) - s * h * (1.0 / 24.0) + pp * (1.0 / 120.0),
            w2[1] + p * w4[1] * (1.0 / 6.0) + s * (1.0 / 24.0),
        )
        x2 = w3[0] * 0.5 + p * (1.0 / 24.0), w3[1] * 0.5 + p * h * (1.0 / 24.0) + s * (1.0 / 120.0)
        gh = slope(*[(-x[1], x[0]) for x in (x0, x1, x2)])
        d2 = scaled(f2, d)
        back = dagger(d2)
        half = 0.5 * (d2[0] + back[0]), 0.5 * (d2[1] + back[1])
        n = mul(b, half)
        d1 = scaled(f1, d)
        whole = (
            d1[0] - 2.0 * n[0] - gp * b[0] - gs * bb[1],
            d1[1] - 2.0 * n[1] - gp * b[1] + gs * bb[0],
        )
        parts = skew_parts(whole)
        shift = (gh - (parts[0] + parts[1] + parts[2])) * (1.0 / 3.0)
        parts = jnp.stack([WEIGHT * (v + shift) for v in parts[:3]] + [WEIGHT * v for v in parts[3:]])
        omega[k] = parts
        return carry

    lax.fori_loop(0, 2, block, 0)


def direct_forces(staple_sum, force, keep_e, omega, direct):
    def block(k):
        own = mul_dn(split(keep_e[k]), split(force[k]))
        direct[k] = join(sub(own, mul(skew_matrix(omega[k]), split(staple_sum[k]))))

    each(0, 2, block)


def kernel(counts, base_hbm, smeared_hbm, force_hbm, out_ref, links, force, csum, direct, ga, gb, gc, gd, wa, wb, wc, wd,
           keep_t, keep_z, sa, sd, keep_n, zb, pa, pb, pc, pd, rim, keep_b, keep_bb, keep_e, keep_s, keep_d, omega,
           recv_u, corner_u, send_w, recv_w, corner_w, in_sem, send_u_sem, recv_u_sem, send_w_sem, recv_w_sem):
    n_gz, n_ta = counts
    gz, ta = lax.axis_index("gz"), lax.axis_index("ta")
    zp, zm = lax.rem(gz + 1, n_gz), lax.rem(gz + n_gz - 1, n_gz)
    tp, tm = lax.rem(ta + 1, n_ta), lax.rem(ta + n_ta - 1, n_ta)
    where = ((zp, ta), (zm, ta), (gz, tp), (gz, tm), (zp, tm), (zm, tp))

    barrier = pltpu.get_barrier_semaphore()
    for device in where:
        pl.semaphore_signal(barrier, inc=1, device_id=device, device_id_type=MESH)

    def fetch(src, dst, slot):
        return [
            pltpu.make_async_copy(src.at[k], dst.at[k // 2, :, pl.ds(k % 2 * 4, 4)], in_sem.at[slot, k])
            for k in range(4)
        ]

    fetches = fetch(smeared_hbm, links.at[0], 0) + fetch(base_hbm, links.at[1], 1) + fetch(force_hbm, force, 2)
    for copy in fetches:
        copy.start()
    m = masks()
    moves_u = [
        link_copies(
            src, recv_u.at[level], corner_u.at[level], (send_u_sem.at[level], recv_u_sem.at[level]), where
        )
        for level, src in ((0, smeared_hbm), (1, base_hbm))
    ]
    pl.semaphore_wait(barrier, 6)
    start(moves_u[0])
    for copy in fetches:
        copy.wait()

    def of(level, *refs):
        return [r.at[level] for r in refs]

    def sent(moves):
        for copy in moves[0] + moves[1]:
            copy.wait_send()

    def landed(copies):
        for copy in copies:
            copy.wait_recv()

    def before(level):
        la, lb, ld, lt = of(level, ga, gb, gd, keep_t)
        gather_own(m, links[level, 0], links[level, 1], la, lb, ld)
        staples_own(la, lb, ld, lt, pc.at[level])

    def forward_ahead(level):
        la, lb, lc, ld, lt, lz = of(level, ga, gb, gc, gd, keep_t, keep_z)
        landed(moves_u[level][0])
        gather_ahead(m, recv_u.at[level], la, lb, lc, ld)
        staples_ahead(la, lb, lc, ld, lt, lz, sa.at[level], pb, pc.at[level], sd.at[level])
        csum[level, 0], csum[level, 1] = scatter_own(m, sa.at[level], pb, pc.at[level], sd.at[level])

    def forward_behind(level):
        la, lb, ld, lt = of(level, ga, gb, gd, keep_t)
        behind = moves_u[level][1]
        landed(behind)
        gather_behind(m, recv_u.at[level], corner_u.at[level], la, lb, ld)
        staples_behind(la, lb, ld, lt, rim)
        low, high = scatter_rim(m, rim)
        csum[level, 0] += low
        csum[level, 1] += high
        exponent_parts(links.at[level], csum.at[level], *of(level, keep_b, keep_bb, keep_e, keep_s))

    def send_force(level):
        exponent_forces(keep_d, *of(level, keep_b, keep_bb, keep_s, omega))
        pack_sends(m, omega[level, 0], omega[level, 1], SKEW, send_w.at[level])
        moves = term_copies(
            omega.at[level], send_w.at[level], recv_w.at[level], corner_w.at[level],
            (send_w_sem.at[level], recv_w_sem.at[level]), where,
        )
        start(moves)
        return moves

    def finish(level, moves, meanwhile):
        la, lb, lc, ld, lt, lz = of(level, ga, gb, gc, gd, keep_t, keep_z)
        direct_forces(csum.at[level], force, keep_e.at[level], omega.at[level], direct)
        gather_own(m, omega[level, 0], omega[level, 1], wa, wb, wd)
        forces_own(la, lb, ld, lt, lz, sa.at[level], sd.at[level], wa, wb, wd, keep_n, zb, pa, pc.at[level], pd)
        meanwhile()
        ahead, behind = moves
        landed(ahead)
        gather_ahead(m, recv_w.at[level], wa, wb, wc, wd)
        forces_ahead(la, lb, lc, ld, lt, lz, wb, wc, keep_n, zb, pa, pb, pc.at[level], pd)
        low, high = scatter_own(m, pa, pb, pc.at[level], pd)
        direct[0] += low
        direct[1] += high
        landed(behind)
        gather_behind(m, recv_w.at[level], corner_w.at[level], wa, wb, wd)
        forces_behind(la, lb, ld, lt, wa, wb, wd, rim)
        low, high = scatter_rim(m, rim)
        low, high = low + direct[0], high + direct[1]
        if level == 0:
            force[0], force[1] = low, high
        else:
            out_ref[0], out_ref[1] = low[:, :4], low[:, 4:]
            out_ref[2], out_ref[3] = high[:, :4], high[:, 4:]

    force_products(links.at[0], force, keep_d)
    before(0)
    before(1)
    sent(moves_u[0])
    start(moves_u[1])
    forward_ahead(0)
    forward_behind(0)
    moves_w0 = send_force(0)
    finish(0, moves_w0, lambda: (forward_ahead(1), forward_behind(1)))
    force_products(links.at[1], force, keep_d)
    moves_w1 = send_force(1)
    finish(1, moves_w1, lambda: None)
    for moves in (moves_u[1], moves_w0, moves_w1):
        sent(moves)


def solution(mesh):
    counts = (mesh.shape["gz"], mesh.shape["ta"])

    def vmem(*shape):
        return pltpu.VMEM(shape + (8, LANES), jnp.float32)

    def per_device(base_links, smeared_links, top_force):
        def flat(v):
            return v.reshape(4, LINK, 4, LANES)

        out = pl.pallas_call(
            lambda *refs: kernel(counts, *refs),
            out_shape=jax.ShapeDtypeStruct((4, LINK, 4, LANES), jnp.float32),
            in_specs=[pl.BlockSpec(memory_space=pl.ANY)] * 3,
            out_specs=pl.BlockSpec(memory_space=pltpu.VMEM),
            scratch_shapes=[
                vmem(2, 2, LINK),
                vmem(2, LINK),
                vmem(2, 2, LINK),
                vmem(2, LINK),
                vmem(2, 5, LINK),
                vmem(2, 5, LINK),
                vmem(2, 3, LINK),
                vmem(2, 5, LINK),
                vmem(5, SKEW),
                vmem(5, SKEW),
                vmem(3, SKEW),
                vmem(5, SKEW),
                vmem(2, 5, LINK),
                vmem(2, 3, LINK),
                vmem(2, 3, LINK),
                vmem(2, 3, LINK),
                vmem(3, LINK),
                vmem(3, LINK),
                vmem(3, LINK),
                vmem(3, LINK),
                vmem(2, 3, LINK),
                vmem(3, LINK),
                vmem(2, LINK),
                vmem(2, 2, SKEW),
                vmem(2, 2, LINK),
                vmem(2, 2, LINK),
                vmem(2, 2, 7),
                vmem(2, LINK),
                vmem(2, 2, SKEW),
                vmem(2, 4, LINK),
                vmem(2, LINK),
                vmem(2, 4, SKEW),
                vmem(2, 4, SKEW),
                vmem(2, SKEW),
                pltpu.SemaphoreType.DMA((3, 4)),
                pltpu.SemaphoreType.DMA((2, 23)),
                pltpu.SemaphoreType.DMA((2, 23)),
                pltpu.SemaphoreType.DMA((2, 7)),
                pltpu.SemaphoreType.DMA((2, 7)),
            ],
            compiler_params=pltpu.CompilerParams(
                collective_id=0, has_side_effects=True, vmem_limit_bytes=48 * 1024 * 1024
            ),
            name="stout_back",
        )(*[pltpu.with_memory_space_constraint(flat(v), pltpu.HBM) for v in (base_links, smeared_links, top_force)])
        return out.reshape(base_links.shape)

    spec = P(None, None, None, None, "gz", "ta", None)
    return jax.shard_map(per_device, mesh=mesh, in_specs=(spec, spec, spec), out_specs=spec, check_vma=False)
```

```python
import jax
import jax.numpy as jnp
from jax import lax
from jax.experimental import pallas as pl
from jax.experimental.pallas import tpu as pltpu
from jax.sharding import PartitionSpec as P

MESH = pl.DeviceIdType.MESH
LY = 8
WEIGHT = 0.1
LANES = 128
LINK = 18
SKEW = 9


def masks():
    row = lax.broadcasted_iota(jnp.int32, (1, 8, LANES), 1)
    col = lax.broadcasted_iota(jnp.int32, (1, 8, LANES), 2) % LY
    return {
        "low": row < 4,
        "even": row % 2 == 0,
        "near": row % 4 < 2,
        "row": row,
        "first": col == 0,
        "last": col == LY - 1,
    }


def pick(mask, yes, no):
    return jnp.where(jnp.broadcast_to(mask, yes.shape), yes, no)


def rows(v, shift):
    return pltpu.roll(v, shift % 8, 1)


def fwd_x(v):
    return pltpu.roll(v, LANES - LY, 2)


def back_x(v):
    return pltpu.roll(v, LY, 2)


def fwd_y(m, v):
    return pick(m["last"], pltpu.roll(v, LY - 1, 2), pltpu.roll(v, LANES - 1, 2))


def back_y(m, v):
    return pick(m["first"], pltpu.roll(v, LANES - LY + 1, 2), pltpu.roll(v, 1, 2))


def fwd_xy(m, v):
    return pick(m["low"], fwd_x(v), fwd_y(m, v))


def back_xy(m, v):
    return pick(m["low"], back_x(v), back_y(m, v))


def split(v):
    return v[:9].reshape(3, 3, 8, LANES), v[9:].reshape(3, 3, 8, LANES)


def join(m):
    return jnp.concatenate([m[0].reshape(9, 8, LANES), m[1].reshape(9, 8, LANES)], axis=0)


def outer_sum(lefts, rights):
    total = None
    for left, right in zip(lefts, rights):
        term = left[:, None] * right[None, :]
        total = term if total is None else total + term
    return total


def columns(a):
    return [a[:, k] for k in range(3)]


def lines(a):
    return [a[k] for k in range(3)]


def product(left, right, sl, sr):
    (ar, ai), (br, bi) = left, right
    rr, ii = outer_sum(ar, br), outer_sum(ai, bi)
    ri, ir = outer_sum(ar, bi), outer_sum(ai, br)
    re = rr - ii if sl * sr > 0 else rr + ii
    if sl > 0 and sr > 0:
        im = ri + ir
    elif sl < 0 and sr > 0:
        im = ri - ir
    else:
        im = ir - ri
    return re, im


def mul(a, b):
    return product((columns(a[0]), columns(a[1])), (lines(b[0]), lines(b[1])), 1, 1)


def mul_dn(a, b):
    return product((lines(a[0]), lines(a[1])), (lines(b[0]), lines(b[1])), -1, 1)


def mul_nd(a, b):
    return product((columns(a[0]), columns(a[1])), (columns(b[0]), columns(b[1])), 1, -1)


def add(a, b):
    return a[0] + b[0], a[1] + b[1]


def sub(a, b):
    return a[0] - b[0], a[1] - b[1]


def flip(v):
    return jnp.stack([v[:, 0], v[:, 1], v[:, 2]], axis=0)


def dagger(a):
    return flip(a[0]), -flip(a[1])


def scaled(c, a):
    cr, ci = c
    return cr * a[0] - ci * a[1], cr * a[1] + ci * a[0]


def skew_parts(a):
    re, im = a
    out = [im[0, 0], im[1, 1], im[2, 2]]
    for i, j in ((0, 1), (0, 2), (1, 2)):
        out += [0.5 * (re[i, j] - re[j, i]), 0.5 * (im[i, j] + im[j, i])]
    return out


def skew_matrix(v):
    d0, d1, d2, r01, i01, r02, i02, r12, i12 = [v[k] for k in range(9)]
    zero = jnp.zeros_like(d0)
    re = jnp.stack([jnp.stack([zero, r01, r02]), jnp.stack([-r01, zero, r12]), jnp.stack([-r02, -r12, zero])])
    im = jnp.stack([jnp.stack([d0, i01, i02]), jnp.stack([i01, d1, i12]), jnp.stack([i02, i12, d2])])
    return re, im


def combine(terms):
    total = None
    for sign, coefficient, vector in terms:
        term = coefficient * vector
        if total is None:
            total = term if sign > 0 else -term
        else:
            total = total + term if sign > 0 else total - term
    return total


def skew_sums(v, xr, xi, side):
    pairs = {(0, 1): (v[3], v[4]), (0, 2): (v[5], v[6]), (1, 2): (v[7], v[8])}
    out_r, out_i = [], []
    for i in range(3):
        re, im = [], []
        for k in range(3):
            if k == i:
                continue
            r, c = pairs[min(i, k), max(i, k)]
            sign = side if i < k else -side
            re += [(sign, r, xr[k]), (-1, c, xi[k])]
            im += [(sign, r, xi[k]), (1, c, xr[k])]
        re = sorted(re, key=lambda t: -t[0]) + [(-1, v[i], xi[i])]
        im = [(1, v[i], xr[i])] + sorted(im, key=lambda t: -t[0])
        out_r.append(combine(re))
        out_i.append(combine(im))
    axis = 0 if side > 0 else 1
    return jnp.stack(out_r, axis=axis), jnp.stack(out_i, axis=axis)


def skew_mul(v, x):
    return skew_sums(v, lines(x[0]), lines(x[1]), 1)


def mul_skew(x, v):
    return skew_sums(v, columns(x[0]), columns(x[1]), -1)


def dn_mul_skew(x, v):
    return skew_sums(v, lines(x[0]), [-c for c in lines(x[1])], -1)


def pack_sends(m, low, high, comps, send):
    send[0, :comps] = pick(m["near"], rows(low, -2), high)
    send[1, :comps] = pick(m["near"], high, rows(low, 2))
    send[2, :comps] = pick(m["even"], rows(low, -1), high)
    send[3, :comps] = pick(m["even"], rows(high, 4), rows(low, 1))


def remote(src, dst, sems, k, device):
    return pltpu.make_async_remote_copy(
        src_ref=src, dst_ref=dst, send_sem=sems[0].at[k], recv_sem=sems[1].at[k], device_id=device, device_id_type=MESH
    )


def link_copies(src, recv, corner, sems, where):
    ahead, behind = [], []
    k = 0

    def put(out, direction, row, count, slot, to):
        nonlocal k
        dst = corner if slot > 3 else recv.at[slot]
        out.append(
            remote(src.at[direction, :, pl.ds(row, count)], dst.at[:, pl.ds(to, count)], sems, k, where[slot])
        )
        k += 1

    put(behind, 2, 2, 1, 4, 1)
    put(behind, 3, 1, 1, 5, 3)
    for direction, to in ((0, 1), (1, 5), (2, 4)):
        put(ahead, direction, 0, 1, 3, to)
        put(ahead, direction, 2, 1, 3, to + 2)
    for direction, to in ((0, 2), (1, 6), (3, 4)):
        put(ahead, direction, 0, 2, 1, to)
    for direction, to in ((0, 0), (2, 1), (1, 4), (3, 5)):
        put(behind, direction, 1, 1, 2, to)
        put(behind, direction, 3, 1, 2, to + 2)
    for direction, to in ((0, 0), (2, 2), (1, 4), (3, 6)):
        put(behind, direction, 2, 2, 0, to)
    return ahead, behind


def term_copies(src, send, recv, corner, sems, where):
    behind = [
        remote(src.at[1, :, pl.ds(2, 1)], corner.at[:, pl.ds(1, 1)], sems, 4, where[4]),
        remote(src.at[1, :, pl.ds(5, 1)], corner.at[:, pl.ds(3, 1)], sems, 5, where[5]),
        remote(send.at[2], recv.at[2], sems, 2, where[2]),
        remote(send.at[0], recv.at[0], sems, 0, where[0]),
    ]
    ahead = [
        remote(send.at[3, :, pl.ds(1, 1)], recv.at[3, :, pl.ds(1, 1)], sems, 3, where[3]),
        remote(send.at[3, :, pl.ds(3, 5)], recv.at[3, :, pl.ds(3, 5)], sems, 6, where[3]),
        remote(send.at[1, :, pl.ds(2, 6)], recv.at[1, :, pl.ds(2, 6)], sems, 1, where[1]),
    ]
    return ahead, behind


def start(moves):
    ahead, behind = moves
    for copy in behind[:2] + ahead + behind[2:]:
        copy.start()


def gather_own(m, low, high, ga, gb, gd):
    ga[0], gd[0] = pick(m["low"], low, rows(high, 4)), pick(m["low"], rows(low, 4), high)
    ga[1], gd[1] = low, high
    gb[1] = fwd_xy(m, high)
    d2 = rows(high, 4)
    ga[2], gd[2] = low, d2
    gb[2] = fwd_xy(m, d2)


def gather_ahead(m, recv, ga, gb, gc, gd):
    at_zp, at_tp = recv[1], recv[3]
    a0, d0, low = ga[0], gd[0], ga[1]
    gb[0] = pick(m["low"], fwd_x(d0), pick(m["near"], rows(d0, -2), rows(at_zp, 2)))
    gc[0] = pick(m["low"], fwd_y(m, a0), pick(m["even"], rows(a0, -1), rows(at_tp, 1)))
    up_z = pick(m["near"], rows(low, -2), at_zp)
    up_t = pick(m["even"], rows(low, -1), at_tp)
    gc[1] = pick(m["low"], up_z, up_t)
    gc[2] = pick(m["low"], up_t, up_z)


def gather_behind(m, recv, corner, ga, gb, gd):
    at_zm, at_tm = recv[0], recv[2]
    diag = corner[...]
    row = m["row"]
    dz = pick(row < 2, rows(at_zm, -2), pick(row < 4, at_zm, pick(row < 6, rows(at_zm, 2), rows(at_zm, 4))))
    ga[3], gd[3] = at_zm, dz
    gb[3] = pick(row < 6, fwd_xy(m, dz), pick(m["even"], rows(at_zm, 3), rows(diag, 6)))
    dt = pick(m["low"], pick(m["even"], rows(at_tm, 3), rows(at_tm, 4)), pick(m["even"], rows(at_tm, -1), at_tm))
    ga[4], gd[4] = at_tm, dt
    gb[4] = pick(m["even"], fwd_xy(m, dt), pick(row < 2, rows(at_tm, 2), diag))


def scatter_own(m, pa, pb, pc, pd):
    a0, b0, c0, d0 = pa[0], pb[0], pc[0], pd[0]
    c1, c2 = pc[1], pc[2]
    zero = jnp.zeros_like(a0)
    from_z = pick(m["near"], zero, rows(pick(m["low"], c1, c2), 2))
    from_t = pick(m["even"], zero, rows(pick(m["low"], c2, c1), 1))
    low = (pa[1] + pa[2]) + (from_z + from_t)
    low = low + pick(m["low"], a0 + back_y(m, c0), rows(d0 + back_x(b0), 4))
    high = (pd[1] + back_xy(m, pb[1])) + rows(pd[2] + back_xy(m, pb[2]), 4)
    z_part = a0 + pick(m["even"], zero, rows(c0, 1))
    t_part = d0 + pick(m["near"], zero, rows(b0, 2))
    return low, high + pick(m["low"], rows(z_part, 4), t_part)


def scatter_rim(m, rim):
    rz, rt = rim[0], rim[1]
    zero = jnp.zeros_like(rz)
    low = pick(m["near"], rz, zero) + pick(m["even"], rt, zero)
    high = pick(m["low"], pick(m["even"], rows(rt, -1), zero), pick(m["near"], rows(rz, -2), zero))
    return low, high


def each(first, last, body):
    def step(k, carry):
        body(k)
        return carry

    lax.fori_loop(first, last, step, 0)


def staples_own(ga, gb, gd, keep_t, pc):
    def corner_products(k):
        keep_t[k] = join(mul_dn(split(ga[k]), split(gd[k])))

    def ends(k):
        pc[k] = join(mul_dn(split(keep_t[k]), split(gb[k])))

    each(0, 3, corner_products)
    each(1, 3, ends)


def staples_ahead(ga, gb, gc, gd, keep_t, keep_z, pa, pb, pc, pd):
    pc[0] = join(mul_dn(split(keep_t[0]), split(gb[0])))

    def block(k):
        c = split(gc[k])
        pb[k] = join(mul(split(keep_t[k]), c))
        z = mul_nd(c, split(gb[k]))
        keep_z[k] = join(z)
        pa[k] = join(mul(split(gd[k]), z))
        pd[k] = join(mul_nd(split(ga[k]), z))

    each(0, 3, block)


def staples_behind(ga, gb, gd, keep_t, rim):
    def block(k):
        t = mul_dn(split(ga[k]), split(gd[k]))
        keep_t[k] = join(t)
        rim[k - 3] = join(mul_dn(t, split(gb[k])))

    each(3, 5, block)


def forces_own(ga, gb, gd, keep_t, keep_z, sa, sd, wa, wb, wd, keep_n, zb, pa, pc, pd):
    def block(k):
        va, vd = wa[k], wd[k]
        keep_n[k] = join(mul_dn(split(ga[k]), skew_mul(va - vd, split(gd[k]))))
        pa[k] = join(skew_mul(vd, split(sa[k])))
        pd[k] = join(skew_mul(va, split(sd[k])))

    each(0, 3, block)
    each(1, 3, lambda k: force_end(gb, keep_t, keep_z, wb, keep_n, zb, pc, k))


def force_end(gb, keep_t, keep_z, wb, keep_n, zb, pc, k):
    ob = wb[k]
    pc[k] = join(mul(sub(dn_mul_skew(split(keep_t[k]), ob), dagger(split(keep_n[k]))), split(gb[k])))
    zb[k] = join(mul_skew(split(keep_z[k]), ob))


def forces_ahead(ga, gb, gc, gd, keep_t, keep_z, wb, wc, keep_n, zb, pa, pb, pc, pd):
    force_end(gb, keep_t, keep_z, wb, keep_n, zb, pc, 0)

    def block(k):
        oc = wc[k]
        pb[k] = join(mul(sub(mul_skew(split(keep_t[k]), oc), split(keep_n[k])), split(gc[k])))
        q = sub(skew_mul(oc, split(keep_z[k])), split(zb[k]))
        pa[k] = join(add(mul(split(gd[k]), q), split(pa[k])))
        pd[k] = join(add(mul_nd(split(ga[k]), q), split(pd[k])))

    each(0, 3, block)


def forces_behind(ga, gb, gd, keep_t, wa, wb, wd, rim):
    def block(k):
        n = mul_dn(split(ga[k]), skew_mul(wa[k] - wd[k], split(gd[k])))
        t = split(keep_t[k])
        rim[k - 3] = join(mul(sub(dn_mul_skew(t, wb[k]), dagger(n)), split(gb[k])))

    each(3, 5, block)


def weights(h):
    hh = h * h
    r2 = 1.0 - hh * 0.5
    r4 = r2 + hh * hh * (1.0 / 24.0)
    r6 = r4 - hh * hh * hh * (1.0 / 720.0)
    i3 = h - h * hh * (1.0 / 6.0)
    i5 = i3 + h * hh * hh * (1.0 / 120.0)
    return (r6, i5), (r4, i5), (r4, i3), (r2, i3), (r2, h)


def exponent_parts(links, staple_sum, keep_b, keep_bb, keep_e, keep_s):
    def block(k, carry):
        u, c = split(links[k]), split(staple_sum[k])
        omega = mul_nd(c, u)
        parts = [WEIGHT * v for v in skew_parts(omega)]
        h = (parts[0] + parts[1] + parts[2]) * (1.0 / 3.0)
        parts = jnp.stack([v - h for v in parts[:3]] + parts[3:])
        b = skew_matrix(parts)
        bb = skew_mul(parts, b)
        p = 0.5 * (bb[0][0, 0] + bb[0][1, 1] + bb[0][2, 2])
        s = jnp.sum((b[1] * bb[0] - b[0] * bb[1]).reshape(9, 8, LANES), axis=0) * (1.0 / 3.0)
        w0, w1, w2, w3, w4 = weights(h)
        pp, ps = p * p, p * s
        f0 = (
            w0[0] - s * w3[1] * (1.0 / 6.0) - ps * h * (1.0 / 120.0) - s * s * (1.0 / 720.0),
            w0[1] + s * w3[0] * (1.0 / 6.0) + ps * (1.0 / 120.0),
        )
        f1 = (
            w1[0] + p * w3[0] * (1.0 / 6.0) - s * w4[1] * (1.0 / 24.0) + pp * (1.0 / 120.0),
            w1[1] + p * w3[1] * (1.0 / 6.0) + s * w4[0] * (1.0 / 24.0) + pp * h * (1.0 / 120.0) + ps * (1.0 / 360.0),
        )
        f2 = (
            w2[0] * 0.5 + p * w4[0] * (1.0 / 24.0) - s * h * (1.0 / 120.0) + pp * (1.0 / 720.0),
            w2[1] * 0.5 + p * w4[1] * (1.0 / 24.0) + s * (1.0 / 120.0),
        )
        e = add(scaled(f1, b), scaled(f2, bb))
        unit = [[jnp.ones_like(p) if i == j else jnp.zeros_like(p) for j in range(3)] for i in range(3)]
        unit = jnp.stack([jnp.stack(r) for r in unit])
        e = e[0] + f0[0] * unit, e[1] + f0[1] * unit
        keep_b[k] = parts
        keep_bb[k] = join(bb)
        keep_e[k] = join(e)
        keep_s[k] = jnp.stack([p, s, h, f1[0], f1[1], f2[0], f2[1]])
        return carry

    lax.fori_loop(0, 2, block, 0)


def force_products(links, force, keep_d):
    def block(k):
        keep_d[k] = join(mul_nd(split(force[k]), split(links[k])))

    each(0, 2, block)


def exponent_forces(keep_d, keep_b, keep_bb, keep_s, omega):
    def block(k, carry):
        b, bb = skew_matrix(keep_b[k]), split(keep_bb[k])
        kept = keep_s[k]
        p, s, h = kept[0], kept[1], kept[2]
        f1, f2 = (kept[3], -kept[4]), (kept[5], -kept[6])
        d = split(keep_d[k])

        def overlap(x):
            re = jnp.sum((d[0] * x[0] + d[1] * x[1]).reshape(9, 8, LANES), axis=0)
            im = jnp.sum((d[0] * x[1] - d[1] * x[0]).reshape(9, 8, LANES), axis=0)
            return re, im

        t0 = d[0][0, 0] + d[0][1, 1] + d[0][2, 2], -(d[1][0, 0] + d[1][1, 1] + d[1][2, 2])
        t1, t2 = overlap(b), overlap(bb)
        w0, w1, w2, w3, w4 = weights(h)
        pp, ps = p * p, p * s

        def slope(*changes):
            total = None
            for t, (re, im) in zip((t0, t1, t2), changes):
                term = t[0] * re - t[1] * im
                total = term if total is None else total + term
            return total

        gp = slope(
            (-s * h * (1.0 / 120.0), s * (1.0 / 120.0)),
            (w3[0] * (1.0 / 6.0) + p * (1.0 / 60.0), w3[1] * (1.0 / 6.0) + p * h * (1.0 / 60.0) + s * (1.0 / 360.0)),
            (w4[0] * (1.0 / 24.0) + p * (1.0 / 360.0), w4[1] * (1.0 / 24.0)),
        )
        gs = slope(
            (
                -w3[1] * (1.0 / 6.0) - p * h * (1.0 / 120.0) - s * (1.0 / 360.0),
                w3[0] * (1.0 / 6.0) + p * (1.0 / 120.0),
            ),
            (-w4[1] * (1.0 / 24.0), w4[0] * (1.0 / 24.0) + p * (1.0 / 360.0)),
            (-h * (1.0 / 120.0), jnp.full_like(h, 1.0 / 120.0)),
        )
        x0 = w1[0] - s * w4[1] * (1.0 / 6.0), w1[1] + s * w4[0] * (1.0 / 6.0) + ps * (1.0 / 120.0)
        x1 = (
            w2[0] + p * w4[0] * (1.0 / 6.0) - s * h * (1.0 / 24.0) + pp * (1.0 / 120.0),
            w2[1] + p * w4[1] * (1.0 / 6.0) + s * (1.0 / 24.0),
        )
        x2 = w3[0] * 0.5 + p * (1.0 / 24.0), w3[1] * 0.5 + p * h * (1.0 / 24.0) + s * (1.0 / 120.0)
        gh = slope(*[(-x[1], x[0]) for x in (x0, x1, x2)])
        d2 = scaled(f2, d)
        back = dagger(d2)
        half = 0.5 * (d2[0] + back[0]), 0.5 * (d2[1] + back[1])
        n = skew_mul(keep_b[k], half)
        d1 = scaled(f1, d)
        whole = (
            d1[0] - 2.0 * n[0] - gp * b[0] - gs * bb[1],
            d1[1] - 2.0 * n[1] - gp * b[1] + gs * bb[0],
        )
        parts = skew_parts(whole)
        shift = (gh - (parts[0] + parts[1] + parts[2])) * (1.0 / 3.0)
        parts = jnp.stack([WEIGHT * (v + shift) for v in parts[:3]] + [WEIGHT * v for v in parts[3:]])
        omega[k] = parts
        return carry

    lax.fori_loop(0, 2, block, 0)


def direct_forces(staple_sum, force, keep_e, omega, direct):
    def block(k):
        own = mul_dn(split(keep_e[k]), split(force[k]))
        direct[k] = join(sub(own, skew_mul(omega[k], split(staple_sum[k]))))

    each(0, 2, block)


def kernel(counts, base_hbm, smeared_hbm, force_hbm, out_ref, links, force, csum, direct, ga, gb, gc, gd, wa, wb, wc, wd,
           keep_t, keep_z, sa, sd, keep_n, zb, pa, pb, pc, pd, rim, keep_b, keep_bb, keep_e, keep_s, keep_d, omega,
           recv_u, corner_u, send_w, recv_w, corner_w, in_sem, send_u_sem, recv_u_sem, send_w_sem, recv_w_sem):
    n_gz, n_ta = counts
    gz, ta = lax.axis_index("gz"), lax.axis_index("ta")
    zp, zm = lax.rem(gz + 1, n_gz), lax.rem(gz + n_gz - 1, n_gz)
    tp, tm = lax.rem(ta + 1, n_ta), lax.rem(ta + n_ta - 1, n_ta)
    where = ((zp, ta), (zm, ta), (gz, tp), (gz, tm), (zp, tm), (zm, tp))

    barrier = pltpu.get_barrier_semaphore()
    for device in where:
        pl.semaphore_signal(barrier, inc=1, device_id=device, device_id_type=MESH)

    def fetch(src, dst, slot):
        return [
            pltpu.make_async_copy(src.at[k], dst.at[k // 2, :, pl.ds(k % 2 * 4, 4)], in_sem.at[slot, k])
            for k in range(4)
        ]

    fetches = fetch(smeared_hbm, links.at[0], 0) + fetch(base_hbm, links.at[1], 1) + fetch(force_hbm, force, 2)
    for copy in fetches:
        copy.start()
    m = masks()
    moves_u = [
        link_copies(
            src, recv_u.at[level], corner_u.at[level], (send_u_sem.at[level], recv_u_sem.at[level]), where
        )
        for level, src in ((0, smeared_hbm), (1, base_hbm))
    ]
    pl.semaphore_wait(barrier, 6)
    start(moves_u[0])
    for copy in fetches:
        copy.wait()

    def of(level, *refs):
        return [r.at[level] for r in refs]

    def sent(moves):
        for copy in moves[0] + moves[1]:
            copy.wait_send()

    def landed(copies):
        for copy in copies:
            copy.wait_recv()

    def before(level):
        la, lb, ld, lt = of(level, ga, gb, gd, keep_t)
        gather_own(m, links[level, 0], links[level, 1], la, lb, ld)
        staples_own(la, lb, ld, lt, pc.at[level])

    def forward_ahead(level):
        la, lb, lc, ld, lt, lz = of(level, ga, gb, gc, gd, keep_t, keep_z)
        landed(moves_u[level][0])
        gather_ahead(m, recv_u.at[level], la, lb, lc, ld)
        staples_ahead(la, lb, lc, ld, lt, lz, sa.at[level], pb, pc.at[level], sd.at[level])
        csum[level, 0], csum[level, 1] = scatter_own(m, sa.at[level], pb, pc.at[level], sd.at[level])

    def forward_behind(level):
        la, lb, ld, lt = of(level, ga, gb, gd, keep_t)
        behind = moves_u[level][1]
        landed(behind)
        gather_behind(m, recv_u.at[level], corner_u.at[level], la, lb, ld)
        staples_behind(la, lb, ld, lt, rim)
        low, high = scatter_rim(m, rim)
        csum[level, 0] += low
        csum[level, 1] += high
        exponent_parts(links.at[level], csum.at[level], *of(level, keep_b, keep_bb, keep_e, keep_s))

    def send_force(level):
        exponent_forces(keep_d, *of(level, keep_b, keep_bb, keep_s, omega))
        pack_sends(m, omega[level, 0], omega[level, 1], SKEW, send_w.at[level])
        moves = term_copies(
            omega.at[level], send_w.at[level], recv_w.at[level], corner_w.at[level],
            (send_w_sem.at[level], recv_w_sem.at[level]), where,
        )
        start(moves)
        return moves

    def finish(level, moves, meanwhile):
        la, lb, lc, ld, lt, lz = of(level, ga, gb, gc, gd, keep_t, keep_z)
        direct_forces(csum.at[level], force, keep_e.at[level], omega.at[level], direct)
        gather_own(m, omega[level, 0], omega[level, 1], wa, wb, wd)
        forces_own(la, lb, ld, lt, lz, sa.at[level], sd.at[level], wa, wb, wd, keep_n, zb, pa, pc.at[level], pd)
        meanwhile()
        ahead, behind = moves
        landed(ahead)
        gather_ahead(m, recv_w.at[level], wa, wb, wc, wd)
        forces_ahead(la, lb, lc, ld, lt, lz, wb, wc, keep_n, zb, pa, pb, pc.at[level], pd)
        low, high = scatter_own(m, pa, pb, pc.at[level], pd)
        direct[0] += low
        direct[1] += high
        landed(behind)
        gather_behind(m, recv_w.at[level], corner_w.at[level], wa, wb, wd)
        forces_behind(la, lb, ld, lt, wa, wb, wd, rim)
        low, high = scatter_rim(m, rim)
        low, high = low + direct[0], high + direct[1]
        if level == 0:
            force[0], force[1] = low, high
        else:
            out_ref[0], out_ref[1] = low[:, :4], low[:, 4:]
            out_ref[2], out_ref[3] = high[:, :4], high[:, 4:]

    force_products(links.at[0], force, keep_d)
    before(0)
    before(1)
    sent(moves_u[0])
    start(moves_u[1])
    forward_ahead(0)
    forward_behind(0)
    moves_w0 = send_force(0)
    finish(0, moves_w0, lambda: (forward_ahead(1), forward_behind(1)))
    force_products(links.at[1], force, keep_d)
    moves_w1 = send_force(1)
    finish(1, moves_w1, lambda: None)
    for moves in (moves_u[1], moves_w0, moves_w1):
        sent(moves)


def solution(mesh):
    counts = (mesh.shape["gz"], mesh.shape["ta"])

    def vmem(*shape):
        return pltpu.VMEM(shape + (8, LANES), jnp.float32)

    def per_device(base_links, smeared_links, top_force):
        def flat(v):
            return v.reshape(4, LINK, 4, LANES)

        out = pl.pallas_call(
            lambda *refs: kernel(counts, *refs),
            out_shape=jax.ShapeDtypeStruct((4, LINK, 4, LANES), jnp.float32),
            in_specs=[pl.BlockSpec(memory_space=pl.ANY)] * 3,
            out_specs=pl.BlockSpec(memory_space=pltpu.VMEM),
            scratch_shapes=[
                vmem(2, 2, LINK),
                vmem(2, LINK),
                vmem(2, 2, LINK),
                vmem(2, LINK),
                vmem(2, 5, LINK),
                vmem(2, 5, LINK),
                vmem(2, 3, LINK),
                vmem(2, 5, LINK),
                vmem(5, SKEW),
                vmem(5, SKEW),
                vmem(3, SKEW),
                vmem(5, SKEW),
                vmem(2, 5, LINK),
                vmem(2, 3, LINK),
                vmem(2, 3, LINK),
                vmem(2, 3, LINK),
                vmem(3, LINK),
                vmem(3, LINK),
                vmem(3, LINK),
                vmem(3, LINK),
                vmem(2, 3, LINK),
                vmem(3, LINK),
                vmem(2, LINK),
                vmem(2, 2, SKEW),
                vmem(2, 2, LINK),
                vmem(2, 2, LINK),
                vmem(2, 2, 7),
                vmem(2, LINK),
                vmem(2, 2, SKEW),
                vmem(2, 4, LINK),
                vmem(2, LINK),
                vmem(2, 4, SKEW),
                vmem(2, 4, SKEW),
                vmem(2, SKEW),
                pltpu.SemaphoreType.DMA((3, 4)),
                pltpu.SemaphoreType.DMA((2, 23)),
                pltpu.SemaphoreType.DMA((2, 23)),
                pltpu.SemaphoreType.DMA((2, 7)),
                pltpu.SemaphoreType.DMA((2, 7)),
            ],
            compiler_params=pltpu.CompilerParams(
                collective_id=0, has_side_effects=True, vmem_limit_bytes=48 * 1024 * 1024
            ),
            name="stout_back",
        )(*[pltpu.with_memory_space_constraint(flat(v), pltpu.HBM) for v in (base_links, smeared_links, top_force)])
        return out.reshape(base_links.shape)

    spec = P(None, None, None, None, "gz", "ta", None)
    return jax.shard_map(per_device, mesh=mesh, in_specs=(spec, spec, spec), out_specs=spec, check_vma=False)
```

```python
import jax
import jax.numpy as jnp
from jax import lax
from jax.experimental import pallas as pl
from jax.experimental.pallas import tpu as pltpu
from jax.sharding import PartitionSpec as P

MESH = pl.DeviceIdType.MESH
LY = 8
WEIGHT = 0.1
LANES = 128
LINK = 18
SKEW = 9


def masks():
    row = lax.broadcasted_iota(jnp.int32, (1, 8, LANES), 1)
    col = lax.broadcasted_iota(jnp.int32, (1, 8, LANES), 2) % LY
    return {
        "low": row < 4,
        "even": row % 2 == 0,
        "near": row % 4 < 2,
        "row": row,
        "first": col == 0,
        "last": col == LY - 1,
    }


def pick(mask, yes, no):
    return jnp.where(jnp.broadcast_to(mask, yes.shape), yes, no)


def rows(v, shift):
    return pltpu.roll(v, shift % 8, 1)


def fwd_x(v):
    return pltpu.roll(v, LANES - LY, 2)


def back_x(v):
    return pltpu.roll(v, LY, 2)


def fwd_y(m, v):
    return pick(m["last"], pltpu.roll(v, LY - 1, 2), pltpu.roll(v, LANES - 1, 2))


def back_y(m, v):
    return pick(m["first"], pltpu.roll(v, LANES - LY + 1, 2), pltpu.roll(v, 1, 2))


def fwd_xy(m, v):
    return pick(m["low"], fwd_x(v), fwd_y(m, v))


def back_xy(m, v):
    return pick(m["low"], back_x(v), back_y(m, v))


def split(v):
    return v[:9].reshape(3, 3, 8, LANES), v[9:].reshape(3, 3, 8, LANES)


def join(m):
    return jnp.concatenate([m[0].reshape(9, 8, LANES), m[1].reshape(9, 8, LANES)], axis=0)


def outer_sum(lefts, rights):
    total = None
    for left, right in zip(lefts, rights):
        term = left[:, None] * right[None, :]
        total = term if total is None else total + term
    return total


def columns(a):
    return [a[:, k] for k in range(3)]


def lines(a):
    return [a[k] for k in range(3)]


def product(left, right, sl, sr):
    (ar, ai), (br, bi) = left, right
    rr, ii = outer_sum(ar, br), outer_sum(ai, bi)
    ri, ir = outer_sum(ar, bi), outer_sum(ai, br)
    re = rr - ii if sl * sr > 0 else rr + ii
    if sl > 0 and sr > 0:
        im = ri + ir
    elif sl < 0 and sr > 0:
        im = ri - ir
    else:
        im = ir - ri
    return re, im


def mul(a, b):
    return product((columns(a[0]), columns(a[1])), (lines(b[0]), lines(b[1])), 1, 1)


def mul_dn(a, b):
    return product((lines(a[0]), lines(a[1])), (lines(b[0]), lines(b[1])), -1, 1)


def mul_nd(a, b):
    return product((columns(a[0]), columns(a[1])), (columns(b[0]), columns(b[1])), 1, -1)


def add(a, b):
    return a[0] + b[0], a[1] + b[1]


def sub(a, b):
    return a[0] - b[0], a[1] - b[1]


def flip(v):
    return jnp.stack([v[:, 0], v[:, 1], v[:, 2]], axis=0)


def dagger(a):
    return flip(a[0]), -flip(a[1])


def scaled(c, a):
    cr, ci = c
    return cr * a[0] - ci * a[1], cr * a[1] + ci * a[0]


def skew_parts(a):
    re, im = a
    out = [im[0, 0], im[1, 1], im[2, 2]]
    for i, j in ((0, 1), (0, 2), (1, 2)):
        out += [0.5 * (re[i, j] - re[j, i]), 0.5 * (im[i, j] + im[j, i])]
    return out


def skew_matrix(v):
    d0, d1, d2, r01, i01, r02, i02, r12, i12 = [v[k] for k in range(9)]
    zero = jnp.zeros_like(d0)
    re = jnp.stack([jnp.stack([zero, r01, r02]), jnp.stack([-r01, zero, r12]), jnp.stack([-r02, -r12, zero])])
    im = jnp.stack([jnp.stack([d0, i01, i02]), jnp.stack([i01, d1, i12]), jnp.stack([i02, i12, d2])])
    return re, im


def combine(terms):
    total = None
    for sign, coefficient, vector in terms:
        term = coefficient * vector
        if total is None:
            total = term if sign > 0 else -term
        else:
            total = total + term if sign > 0 else total - term
    return total


def skew_sums(v, xr, xi, side):
    pairs = {(0, 1): (v[3], v[4]), (0, 2): (v[5], v[6]), (1, 2): (v[7], v[8])}
    out_r, out_i = [], []
    for i in range(3):
        re, im = [], []
        for k in range(3):
            if k == i:
                continue
            r, c = pairs[min(i, k), max(i, k)]
            sign = side if i < k else -side
            re += [(sign, r, xr[k]), (-1, c, xi[k])]
            im += [(sign, r, xi[k]), (1, c, xr[k])]
        re = sorted(re, key=lambda t: -t[0]) + [(-1, v[i], xi[i])]
        im = [(1, v[i], xr[i])] + sorted(im, key=lambda t: -t[0])
        out_r.append(combine(re))
        out_i.append(combine(im))
    axis = 0 if side > 0 else 1
    return jnp.stack(out_r, axis=axis), jnp.stack(out_i, axis=axis)


def skew_mul(v, x):
    return skew_sums(v, lines(x[0]), lines(x[1]), 1)


def mul_skew(x, v):
    return skew_sums(v, columns(x[0]), columns(x[1]), -1)


def dn_mul_skew(x, v):
    return skew_sums(v, lines(x[0]), [-c for c in lines(x[1])], -1)


def pack_sends(m, low, high, comps, send):
    send[0, :comps] = pick(m["near"], rows(low, -2), high)
    send[1, :comps] = pick(m["near"], high, rows(low, 2))
    send[2, :comps] = pick(m["even"], rows(low, -1), high)
    send[3, :comps] = pick(m["even"], rows(high, 4), rows(low, 1))


def remote(src, dst, sems, k, device):
    return pltpu.make_async_remote_copy(
        src_ref=src, dst_ref=dst, send_sem=sems[0].at[k], recv_sem=sems[1].at[k], device_id=device, device_id_type=MESH
    )


def link_copies(src, recv, corner, sems, where):
    ahead, behind = [], []
    k = 0

    def put(out, direction, row, count, slot, to):
        nonlocal k
        dst = corner if slot > 3 else recv.at[slot]
        out.append(
            remote(src.at[direction, :, pl.ds(row, count)], dst.at[:, pl.ds(to, count)], sems, k, where[slot])
        )
        k += 1

    put(behind, 2, 2, 1, 4, 1)
    put(behind, 3, 1, 1, 5, 3)
    for direction, to in ((0, 1), (1, 5), (2, 4)):
        put(ahead, direction, 0, 1, 3, to)
        put(ahead, direction, 2, 1, 3, to + 2)
    for direction, to in ((0, 2), (1, 6), (3, 4)):
        put(ahead, direction, 0, 2, 1, to)
    for direction, to in ((0, 0), (2, 1), (1, 4), (3, 5)):
        put(behind, direction, 1, 1, 2, to)
        put(behind, direction, 3, 1, 2, to + 2)
    for direction, to in ((0, 0), (2, 2), (1, 4), (3, 6)):
        put(behind, direction, 2, 2, 0, to)
    return ahead, behind


def term_copies(src, send, recv, corner, sems, where):
    behind = [
        remote(src.at[1, :, pl.ds(2, 1)], corner.at[:, pl.ds(1, 1)], sems, 4, where[4]),
        remote(src.at[1, :, pl.ds(5, 1)], corner.at[:, pl.ds(3, 1)], sems, 5, where[5]),
        remote(send.at[2], recv.at[2], sems, 2, where[2]),
        remote(send.at[0], recv.at[0], sems, 0, where[0]),
    ]
    ahead = [
        remote(send.at[3, :, pl.ds(1, 1)], recv.at[3, :, pl.ds(1, 1)], sems, 3, where[3]),
        remote(send.at[3, :, pl.ds(3, 5)], recv.at[3, :, pl.ds(3, 5)], sems, 6, where[3]),
        remote(send.at[1, :, pl.ds(2, 6)], recv.at[1, :, pl.ds(2, 6)], sems, 1, where[1]),
    ]
    return ahead, behind


def start(moves):
    ahead, behind = moves
    for copy in behind[:2] + ahead + behind[2:]:
        copy.start()


def gather_own(m, low, high, ga, gb, gd):
    ga[0], gd[0] = pick(m["low"], low, rows(high, 4)), pick(m["low"], rows(low, 4), high)
    ga[1], gd[1] = low, high
    gb[1] = fwd_xy(m, high)
    d2 = rows(high, 4)
    ga[2], gd[2] = low, d2
    gb[2] = fwd_xy(m, d2)


def gather_ahead(m, recv, ga, gb, gc, gd):
    at_zp, at_tp = recv[1], recv[3]
    a0, d0, low = ga[0], gd[0], ga[1]
    gb[0] = pick(m["low"], fwd_x(d0), pick(m["near"], rows(d0, -2), rows(at_zp, 2)))
    gc[0] = pick(m["low"], fwd_y(m, a0), pick(m["even"], rows(a0, -1), rows(at_tp, 1)))
    up_z = pick(m["near"], rows(low, -2), at_zp)
    up_t = pick(m["even"], rows(low, -1), at_tp)
    gc[1] = pick(m["low"], up_z, up_t)
    gc[2] = pick(m["low"], up_t, up_z)


def gather_behind(m, recv, corner, ga, gb, gd):
    at_zm, at_tm = recv[0], recv[2]
    diag = corner[...]
    row = m["row"]
    dz = pick(row < 2, rows(at_zm, -2), pick(row < 4, at_zm, pick(row < 6, rows(at_zm, 2), rows(at_zm, 4))))
    ga[3], gd[3] = at_zm, dz
    gb[3] = pick(row < 6, fwd_xy(m, dz), pick(m["even"], rows(at_zm, 3), rows(diag, 6)))
    dt = pick(m["low"], pick(m["even"], rows(at_tm, 3), rows(at_tm, 4)), pick(m["even"], rows(at_tm, -1), at_tm))
    ga[4], gd[4] = at_tm, dt
    gb[4] = pick(m["even"], fwd_xy(m, dt), pick(row < 2, rows(at_tm, 2), diag))


def scatter_own(m, pa, pb, pc, pd):
    a0, b0, c0, d0 = pa[0], pb[0], pc[0], pd[0]
    c1, c2 = pc[1], pc[2]
    zero = jnp.zeros_like(a0)
    from_z = pick(m["near"], zero, rows(pick(m["low"], c1, c2), 2))
    from_t = pick(m["even"], zero, rows(pick(m["low"], c2, c1), 1))
    low = (pa[1] + pa[2]) + (from_z + from_t)
    low = low + pick(m["low"], a0 + back_y(m, c0), rows(d0 + back_x(b0), 4))
    high = (pd[1] + back_xy(m, pb[1])) + rows(pd[2] + back_xy(m, pb[2]), 4)
    z_part = a0 + pick(m["even"], zero, rows(c0, 1))
    t_part = d0 + pick(m["near"], zero, rows(b0, 2))
    return low, high + pick(m["low"], rows(z_part, 4), t_part)


def scatter_rim(m, rim):
    rz, rt = rim[0], rim[1]
    zero = jnp.zeros_like(rz)
    low = pick(m["near"], rz, zero) + pick(m["even"], rt, zero)
    high = pick(m["low"], pick(m["even"], rows(rt, -1), zero), pick(m["near"], rows(rz, -2), zero))
    return low, high


def each(first, last, body):
    for k in range(first, last):
        body(k)


def staples_own(ga, gb, gd, keep_t, pc):
    def corner_products(k):
        keep_t[k] = join(mul_dn(split(ga[k]), split(gd[k])))

    def ends(k):
        pc[k] = join(mul_dn(split(keep_t[k]), split(gb[k])))

    each(0, 3, corner_products)
    each(1, 3, ends)


def staples_ahead(ga, gb, gc, gd, keep_t, keep_z, pa, pb, pc, pd):
    pc[0] = join(mul_dn(split(keep_t[0]), split(gb[0])))

    def block(k):
        c = split(gc[k])
        pb[k] = join(mul(split(keep_t[k]), c))
        z = mul_nd(c, split(gb[k]))
        keep_z[k] = join(z)
        pa[k] = join(mul(split(gd[k]), z))
        pd[k] = join(mul_nd(split(ga[k]), z))

    each(0, 3, block)


def staples_behind(ga, gb, gd, keep_t, rim):
    def block(k):
        t = mul_dn(split(ga[k]), split(gd[k]))
        keep_t[k] = join(t)
        rim[k - 3] = join(mul_dn(t, split(gb[k])))

    each(3, 5, block)


def forces_own(ga, gb, gd, keep_t, keep_z, sa, sd, wa, wb, wd, keep_n, zb, pa, pc, pd):
    def block(k):
        va, vd = wa[k], wd[k]
        keep_n[k] = join(mul_dn(split(ga[k]), skew_mul(va - vd, split(gd[k]))))
        pa[k] = join(skew_mul(vd, split(sa[k])))
        pd[k] = join(skew_mul(va, split(sd[k])))

    each(0, 3, block)
    each(1, 3, lambda k: force_end(gb, keep_t, keep_z, wb, keep_n, zb, pc, k))


def force_end(gb, keep_t, keep_z, wb, keep_n, zb, pc, k):
    ob = wb[k]
    pc[k] = join(mul(sub(dn_mul_skew(split(keep_t[k]), ob), dagger(split(keep_n[k]))), split(gb[k])))
    zb[k] = join(mul_skew(split(keep_z[k]), ob))


def forces_ahead(ga, gb, gc, gd, keep_t, keep_z, wb, wc, keep_n, zb, pa, pb, pc, pd):
    force_end(gb, keep_t, keep_z, wb, keep_n, zb, pc, 0)

    def block(k):
        oc = wc[k]
        pb[k] = join(mul(sub(mul_skew(split(keep_t[k]), oc), split(keep_n[k])), split(gc[k])))
        q = sub(skew_mul(oc, split(keep_z[k])), split(zb[k]))
        pa[k] = join(add(mul(split(gd[k]), q), split(pa[k])))
        pd[k] = join(add(mul_nd(split(ga[k]), q), split(pd[k])))

    each(0, 3, block)


def forces_behind(ga, gb, gd, keep_t, wa, wb, wd, rim):
    def block(k):
        n = mul_dn(split(ga[k]), skew_mul(wa[k] - wd[k], split(gd[k])))
        t = split(keep_t[k])
        rim[k - 3] = join(mul(sub(dn_mul_skew(t, wb[k]), dagger(n)), split(gb[k])))

    each(3, 5, block)


def weights(h):
    hh = h * h
    r2 = 1.0 - hh * 0.5
    r4 = r2 + hh * hh * (1.0 / 24.0)
    r6 = r4 - hh * hh * hh * (1.0 / 720.0)
    i3 = h - h * hh * (1.0 / 6.0)
    i5 = i3 + h * hh * hh * (1.0 / 120.0)
    return (r6, i5), (r4, i5), (r4, i3), (r2, i3), (r2, h)


def exponent_parts(links, staple_sum, keep_b, keep_bb, keep_e, keep_s):
    def block(k, carry):
        u, c = split(links[k]), split(staple_sum[k])
        omega = mul_nd(c, u)
        parts = [WEIGHT * v for v in skew_parts(omega)]
        h = (parts[0] + parts[1] + parts[2]) * (1.0 / 3.0)
        parts = jnp.stack([v - h for v in parts[:3]] + parts[3:])
        b = skew_matrix(parts)
        bb = skew_mul(parts, b)
        p = 0.5 * (bb[0][0, 0] + bb[0][1, 1] + bb[0][2, 2])
        s = jnp.sum((b[1] * bb[0] - b[0] * bb[1]).reshape(9, 8, LANES), axis=0) * (1.0 / 3.0)
        w0, w1, w2, w3, w4 = weights(h)
        pp, ps = p * p, p * s
        f0 = (
            w0[0] - s * w3[1] * (1.0 / 6.0) - ps * h * (1.0 / 120.0) - s * s * (1.0 / 720.0),
            w0[1] + s * w3[0] * (1.0 / 6.0) + ps * (1.0 / 120.0),
        )
        f1 = (
            w1[0] + p * w3[0] * (1.0 / 6.0) - s * w4[1] * (1.0 / 24.0) + pp * (1.0 / 120.0),
            w1[1] + p * w3[1] * (1.0 / 6.0) + s * w4[0] * (1.0 / 24.0) + pp * h * (1.0 / 120.0) + ps * (1.0 / 360.0),
        )
        f2 = (
            w2[0] * 0.5 + p * w4[0] * (1.0 / 24.0) - s * h * (1.0 / 120.0) + pp * (1.0 / 720.0),
            w2[1] * 0.5 + p * w4[1] * (1.0 / 24.0) + s * (1.0 / 120.0),
        )
        e = add(scaled(f1, b), scaled(f2, bb))
        unit = [[jnp.ones_like(p) if i == j else jnp.zeros_like(p) for j in range(3)] for i in range(3)]
        unit = jnp.stack([jnp.stack(r) for r in unit])
        e = e[0] + f0[0] * unit, e[1] + f0[1] * unit
        keep_b[k] = parts
        keep_bb[k] = join(bb)
        keep_e[k] = join(e)
        keep_s[k] = jnp.stack([p, s, h, f1[0], f1[1], f2[0], f2[1]])
        return carry

    for k in range(2):
        block(k, 0)


def force_products(links, force, keep_d):
    def block(k):
        keep_d[k] = join(mul_nd(split(force[k]), split(links[k])))

    each(0, 2, block)


def exponent_forces(keep_d, keep_b, keep_bb, keep_s, omega):
    def block(k, carry):
        b, bb = skew_matrix(keep_b[k]), split(keep_bb[k])
        kept = keep_s[k]
        p, s, h = kept[0], kept[1], kept[2]
        f1, f2 = (kept[3], -kept[4]), (kept[5], -kept[6])
        d = split(keep_d[k])

        def overlap(x):
            re = jnp.sum((d[0] * x[0] + d[1] * x[1]).reshape(9, 8, LANES), axis=0)
            im = jnp.sum((d[0] * x[1] - d[1] * x[0]).reshape(9, 8, LANES), axis=0)
            return re, im

        t0 = d[0][0, 0] + d[0][1, 1] + d[0][2, 2], -(d[1][0, 0] + d[1][1, 1] + d[1][2, 2])
        t1, t2 = overlap(b), overlap(bb)
        w0, w1, w2, w3, w4 = weights(h)
        pp, ps = p * p, p * s

        def slope(*changes):
            total = None
            for t, (re, im) in zip((t0, t1, t2), changes):
                term = t[0] * re - t[1] * im
                total = term if total is None else total + term
            return total

        gp = slope(
            (-s * h * (1.0 / 120.0), s * (1.0 / 120.0)),
            (w3[0] * (1.0 / 6.0) + p * (1.0 / 60.0), w3[1] * (1.0 / 6.0) + p * h * (1.0 / 60.0) + s * (1.0 / 360.0)),
            (w4[0] * (1.0 / 24.0) + p * (1.0 / 360.0), w4[1] * (1.0 / 24.0)),
        )
        gs = slope(
            (
                -w3[1] * (1.0 / 6.0) - p * h * (1.0 / 120.0) - s * (1.0 / 360.0),
                w3[0] * (1.0 / 6.0) + p * (1.0 / 120.0),
            ),
            (-w4[1] * (1.0 / 24.0), w4[0] * (1.0 / 24.0) + p * (1.0 / 360.0)),
            (-h * (1.0 / 120.0), jnp.full_like(h, 1.0 / 120.0)),
        )
        x0 = w1[0] - s * w4[1] * (1.0 / 6.0), w1[1] + s * w4[0] * (1.0 / 6.0) + ps * (1.0 / 120.0)
        x1 = (
            w2[0] + p * w4[0] * (1.0 / 6.0) - s * h * (1.0 / 24.0) + pp * (1.0 / 120.0),
            w2[1] + p * w4[1] * (1.0 / 6.0) + s * (1.0 / 24.0),
        )
        x2 = w3[0] * 0.5 + p * (1.0 / 24.0), w3[1] * 0.5 + p * h * (1.0 / 24.0) + s * (1.0 / 120.0)
        gh = slope(*[(-x[1], x[0]) for x in (x0, x1, x2)])
        d2 = scaled(f2, d)
        back = dagger(d2)
        half = 0.5 * (d2[0] + back[0]), 0.5 * (d2[1] + back[1])
        n = skew_mul(keep_b[k], half)
        d1 = scaled(f1, d)
        whole = (
            d1[0] - 2.0 * n[0] - gp * b[0] - gs * bb[1],
            d1[1] - 2.0 * n[1] - gp * b[1] + gs * bb[0],
        )
        parts = skew_parts(whole)
        shift = (gh - (parts[0] + parts[1] + parts[2])) * (1.0 / 3.0)
        parts = jnp.stack([WEIGHT * (v + shift) for v in parts[:3]] + [WEIGHT * v for v in parts[3:]])
        omega[k] = parts
        return carry

    for k in range(2):
        block(k, 0)


def direct_forces(staple_sum, force, keep_e, omega, direct):
    def block(k):
        own = mul_dn(split(keep_e[k]), split(force[k]))
        direct[k] = join(sub(own, skew_mul(omega[k], split(staple_sum[k]))))

    each(0, 2, block)


def kernel(counts, base_hbm, smeared_hbm, force_hbm, out_ref, links, force, csum, direct, ga, gb, gc, gd, wa, wb, wc, wd,
           keep_t, keep_z, sa, sd, keep_n, zb, pa, pb, pc, pd, rim, keep_b, keep_bb, keep_e, keep_s, keep_d, omega,
           recv_u, corner_u, send_w, recv_w, corner_w, in_sem, send_u_sem, recv_u_sem, send_w_sem, recv_w_sem):
    n_gz, n_ta = counts
    gz, ta = lax.axis_index("gz"), lax.axis_index("ta")
    zp, zm = lax.rem(gz + 1, n_gz), lax.rem(gz + n_gz - 1, n_gz)
    tp, tm = lax.rem(ta + 1, n_ta), lax.rem(ta + n_ta - 1, n_ta)
    where = ((zp, ta), (zm, ta), (gz, tp), (gz, tm), (zp, tm), (zm, tp))

    barrier = pltpu.get_barrier_semaphore()
    for device in where:
        pl.semaphore_signal(barrier, inc=1, device_id=device, device_id_type=MESH)

    def fetch(src, dst, slot):
        return [
            pltpu.make_async_copy(src.at[k], dst.at[k // 2, :, pl.ds(k % 2 * 4, 4)], in_sem.at[slot, k])
            for k in range(4)
        ]

    fetches = fetch(smeared_hbm, links.at[0], 0) + fetch(base_hbm, links.at[1], 1) + fetch(force_hbm, force, 2)
    for copy in fetches:
        copy.start()
    m = masks()
    moves_u = [
        link_copies(
            src, recv_u.at[level], corner_u.at[level], (send_u_sem.at[level], recv_u_sem.at[level]), where
        )
        for level, src in ((0, smeared_hbm), (1, base_hbm))
    ]
    pl.semaphore_wait(barrier, 6)
    start(moves_u[0])
    for copy in fetches:
        copy.wait()

    def of(level, *refs):
        return [r.at[level] for r in refs]

    def sent(moves):
        for copy in moves[0] + moves[1]:
            copy.wait_send()

    def landed(copies):
        for copy in copies:
            copy.wait_recv()

    def before(level):
        la, lb, ld, lt = of(level, ga, gb, gd, keep_t)
        gather_own(m, links[level, 0], links[level, 1], la, lb, ld)
        staples_own(la, lb, ld, lt, pc.at[level])

    def forward_ahead(level):
        la, lb, lc, ld, lt, lz = of(level, ga, gb, gc, gd, keep_t, keep_z)
        landed(moves_u[level][0])
        gather_ahead(m, recv_u.at[level], la, lb, lc, ld)
        staples_ahead(la, lb, lc, ld, lt, lz, sa.at[level], pb, pc.at[level], sd.at[level])
        csum[level, 0], csum[level, 1] = scatter_own(m, sa.at[level], pb, pc.at[level], sd.at[level])

    def forward_behind(level):
        la, lb, ld, lt = of(level, ga, gb, gd, keep_t)
        behind = moves_u[level][1]
        landed(behind)
        gather_behind(m, recv_u.at[level], corner_u.at[level], la, lb, ld)
        staples_behind(la, lb, ld, lt, rim)
        low, high = scatter_rim(m, rim)
        csum[level, 0] += low
        csum[level, 1] += high
        exponent_parts(links.at[level], csum.at[level], *of(level, keep_b, keep_bb, keep_e, keep_s))

    def send_force(level):
        exponent_forces(keep_d, *of(level, keep_b, keep_bb, keep_s, omega))
        pack_sends(m, omega[level, 0], omega[level, 1], SKEW, send_w.at[level])
        moves = term_copies(
            omega.at[level], send_w.at[level], recv_w.at[level], corner_w.at[level],
            (send_w_sem.at[level], recv_w_sem.at[level]), where,
        )
        start(moves)
        return moves

    def finish(level, moves, meanwhile):
        la, lb, lc, ld, lt, lz = of(level, ga, gb, gc, gd, keep_t, keep_z)
        direct_forces(csum.at[level], force, keep_e.at[level], omega.at[level], direct)
        gather_own(m, omega[level, 0], omega[level, 1], wa, wb, wd)
        forces_own(la, lb, ld, lt, lz, sa.at[level], sd.at[level], wa, wb, wd, keep_n, zb, pa, pc.at[level], pd)
        meanwhile()
        ahead, behind = moves
        landed(ahead)
        gather_ahead(m, recv_w.at[level], wa, wb, wc, wd)
        forces_ahead(la, lb, lc, ld, lt, lz, wb, wc, keep_n, zb, pa, pb, pc.at[level], pd)
        low, high = scatter_own(m, pa, pb, pc.at[level], pd)
        direct[0] += low
        direct[1] += high
        landed(behind)
        gather_behind(m, recv_w.at[level], corner_w.at[level], wa, wb, wd)
        forces_behind(la, lb, ld, lt, wa, wb, wd, rim)
        low, high = scatter_rim(m, rim)
        low, high = low + direct[0], high + direct[1]
        if level == 0:
            force[0], force[1] = low, high
        else:
            out_ref[0], out_ref[1] = low[:, :4], low[:, 4:]
            out_ref[2], out_ref[3] = high[:, :4], high[:, 4:]

    force_products(links.at[0], force, keep_d)
    before(0)
    before(1)
    sent(moves_u[0])
    start(moves_u[1])
    forward_ahead(0)
    forward_behind(0)
    moves_w0 = send_force(0)
    finish(0, moves_w0, lambda: (forward_ahead(1), forward_behind(1)))
    force_products(links.at[1], force, keep_d)
    moves_w1 = send_force(1)
    finish(1, moves_w1, lambda: None)
    for moves in (moves_u[1], moves_w0, moves_w1):
        sent(moves)


def solution(mesh):
    counts = (mesh.shape["gz"], mesh.shape["ta"])

    def vmem(*shape):
        return pltpu.VMEM(shape + (8, LANES), jnp.float32)

    def per_device(base_links, smeared_links, top_force):
        def flat(v):
            return v.reshape(4, LINK, 4, LANES)

        out = pl.pallas_call(
            lambda *refs: kernel(counts, *refs),
            out_shape=jax.ShapeDtypeStruct((4, LINK, 4, LANES), jnp.float32),
            in_specs=[pl.BlockSpec(memory_space=pl.ANY)] * 3,
            out_specs=pl.BlockSpec(memory_space=pltpu.VMEM),
            scratch_shapes=[
                vmem(2, 2, LINK),
                vmem(2, LINK),
                vmem(2, 2, LINK),
                vmem(2, LINK),
                vmem(2, 5, LINK),
                vmem(2, 5, LINK),
                vmem(2, 3, LINK),
                vmem(2, 5, LINK),
                vmem(5, SKEW),
                vmem(5, SKEW),
                vmem(3, SKEW),
                vmem(5, SKEW),
                vmem(2, 5, LINK),
                vmem(2, 3, LINK),
                vmem(2, 3, LINK),
                vmem(2, 3, LINK),
                vmem(3, LINK),
                vmem(3, LINK),
                vmem(3, LINK),
                vmem(3, LINK),
                vmem(2, 3, LINK),
                vmem(3, LINK),
                vmem(2, LINK),
                vmem(2, 2, SKEW),
                vmem(2, 2, LINK),
                vmem(2, 2, LINK),
                vmem(2, 2, 7),
                vmem(2, LINK),
                vmem(2, 2, SKEW),
                vmem(2, 4, LINK),
                vmem(2, LINK),
                vmem(2, 4, SKEW),
                vmem(2, 4, SKEW),
                vmem(2, SKEW),
                pltpu.SemaphoreType.DMA((3, 4)),
                pltpu.SemaphoreType.DMA((2, 23)),
                pltpu.SemaphoreType.DMA((2, 23)),
                pltpu.SemaphoreType.DMA((2, 7)),
                pltpu.SemaphoreType.DMA((2, 7)),
            ],
            compiler_params=pltpu.CompilerParams(
                collective_id=0, has_side_effects=True, vmem_limit_bytes=48 * 1024 * 1024
            ),
            name="stout_back",
        )(*[pltpu.with_memory_space_constraint(flat(v), pltpu.HBM) for v in (base_links, smeared_links, top_force)])
        return out.reshape(base_links.shape)

    spec = P(None, None, None, None, "gz", "ta", None)
    return jax.shard_map(per_device, mesh=mesh, in_specs=(spec, spec, spec), out_specs=spec, check_vma=False)
```
